32 devices in a mesh: seq: 8 (over y, x, core), head: 4 (over z).
Axes of the slice: x: 2, y: 2, z: 4, core: 2. Of those that a mesh axis runs over, the one named last changes fastest.
Arguments:
- queries: bfloat16 [8192, 32, 128], P(('seq', 'head')), may hold values from -6 to 6
- keys: bfloat16 [8192, 32, 2, 128], P(('seq', 'head')), may hold values from -6 to 6
- values: bfloat16 [8192, 32, 2, 128], P(('seq', 'head')), may hold values from -6 to 6
- initial_state: float32 [32, 128, 128], P('head'), may hold values from -192 to 192
Outputs:
- mixed: bfloat16 [8192, 32, 128], P(('seq', 'head'))
The draws below stay inside these ranges and needn't reach their ends.
All inputs are finite; a program needn't handle non-finite values.
Results may differ from the reference program's by a relative error of at most 0.004.
Values may be sent and summed in bfloat16 or wider, within the bound.
A program may use at most 128 MiB of HBM per device.

```python
import jax
import jax.numpy as jnp
from jax import lax

HD = 128
HEADS = 32
UPDATES = 2
TOKENS = 8192


def shard_levels(own_key, dims, shards, smallest, top_value):
    def one(axis_at, shards_of):
        heights = jax.random.uniform(jax.random.fold_in(jax.random.fold_in(own_key, 6), axis_at), (shards_of,), jnp.float32, smallest / len(shards), top_value / len(shards))
        return jnp.repeat(jnp.exp(heights), dims[axis_at] // shards_of).reshape((-1,) + (1,) * (len(dims) - axis_at - 1))

    level = one(*shards[0])
    for cut in shards[1:]:
        level = level * one(*cut)
    return level


def gaussian(rng, extent, scale, bound, split=(), dtype=jnp.bfloat16):
    entries = scale * jax.random.normal(rng, extent, jnp.float32)
    if split:
        entries = entries * shard_levels(rng, extent, split, -0.22, 0.18)
    return jnp.clip(entries, -bound, bound).astype(dtype)


def setup_inputs(seed: int = 0) -> dict:
    arg_keys = jax.random.split(jax.random.key(seed), 5)
    return {
        "queries": gaussian(arg_keys[0], (TOKENS, HEADS, HD), 1.0, 6.0, ((0, 32),)),
        "keys": gaussian(arg_keys[1], (TOKENS, HEADS, UPDATES, HD), 1.0, 6.0, ((0, 32),)),
        "values": gaussian(arg_keys[2], (TOKENS, HEADS, UPDATES, HD), 1.0, 6.0, ((0, 32),)),
        "initial_state": gaussian(arg_keys[3], (HEADS, HD, HD), 32.0, 192.0, ((0, 4),), jnp.float32),
    }


HIGH = lax.Precision.HIGHEST

def unit_rows(raw_keys):
    floats = raw_keys.astype(jnp.float32)
    return floats * lax.rsqrt(lax.optimization_barrier(jnp.sum(floats * floats, axis=-1, keepdims=True)) + 1e-06)

def reference(queries, keys, values, initial_state):
    q_float = queries.astype(jnp.float32)
    k_unit = unit_rows(keys)
    v_float = values.astype(jnp.float32)

    def advance(carry_state, token_item):
        q_now, k_now, v_now = token_item
        for index_j in range(UPDATES):
            key_now = k_now[:, index_j]
            projected = jnp.einsum('hd,hde->he', key_now, carry_state, precision=HIGH)
            carry_state = carry_state + 2.0 * key_now[:, :, None] * (v_now[:, index_j] - projected)[:, None, :]
        return (carry_state, jnp.einsum('hd,hde->he', q_now, carry_state, precision=HIGH))
    final_state, raw_out = lax.scan(advance, initial_state.astype(jnp.float32), (q_float, k_unit, v_float))
    scaled = raw_out * lax.rsqrt(lax.optimization_barrier(jnp.mean(raw_out * raw_out, axis=-1, keepdims=True)) + 1e-06)
    return scaled.astype(jnp.bfloat16)
```

```python
import functools

import jax
import jax.numpy as jnp
from jax import lax
from jax.experimental import pallas as pl
from jax.experimental.pallas import tpu as pltpu
from jax.sharding import PartitionSpec as P

BLOCK = 64
BASE = 16
HEADS_A_STEP = 8
UNIT = 4
VMEM_BYTES = 56 << 20

F32 = jnp.float32
BF16 = jnp.bfloat16
MESH = pl.DeviceIdType.MESH


def mm(left, right, dims=((1,), (0,))):
    return lax.dot_general(left, right, (dims, ((), ())), preferred_element_type=F32)


def split(x):
    high = x.astype(BF16)
    return high, (x - high.astype(F32)).astype(BF16)


def cat(parts, axis):
    return jnp.concatenate(parts, axis=axis)


def exact_left(left, right):
    high, low = split(right)
    return mm(cat([left, left], 1), cat([high, low], 0))


def exact_right(left, right):
    high, low = split(left)
    return mm(cat([high, low], 1), cat([right, right], 0))


def both_split(lh, ll, rh, rl):
    return mm(cat([lh, ll], 1), cat([rh, rh], 0)) + mm(lh, rl)


def both(left, right):
    return both_split(*split(left), *split(right))


def odd_rows(x, size):
    rows = x.shape[0]
    return cat([x[s : s + size] for s in range(size, rows, 2 * size)], 0)


def merge_rows(even_from, odd, size):
    rows = even_from.shape[0]
    parts = []
    for i, s in enumerate(range(0, rows, 2 * size)):
        parts += [even_from[s : s + size], odd[i * size : (i + 1) * size]]
    return cat(parts, 0)


def unit_lower_inverses(xs):
    n = xs[0].shape[0]
    row = lax.broadcasted_iota(jnp.int32, (n, n), 0)
    col = lax.broadcasted_iota(jnp.int32, (n, n), 1)
    same = row // BASE == col // BASE
    sub = lax.broadcasted_iota(jnp.int32, (BASE, n), 0)
    lane = lax.broadcasted_iota(jnp.int32, (BASE, n), 1)
    packs = []
    for x in xs:
        inner = jnp.where(same, x, 0.0)
        packed = inner[:BASE]
        for s in range(BASE, n, BASE):
            packed = packed + inner[s : s + BASE]
        packs.append(packed)
    invs = [jnp.where(sub == lane % BASE, 1.0, 0.0) for _ in xs]
    for j in range(BASE - 1):
        at = lane - lane % BASE + j
        coefs = [jnp.take_along_axis(packed, at, axis=1) for packed in packs]
        invs = [inv - coef * inv[j : j + 1] for inv, coef in zip(invs, coefs)]
    ms = [jnp.where(same, cat([inv] * (n // BASE), 0), 0.0) for inv in invs]
    size = BASE
    while size < n:
        near = col // size == row // size - 1
        belows = [split(odd_rows(jnp.where(near, x, 0.0), size)) for x in xs]
        halves = [split(m) for m in ms]
        ys = [both_split(*below, *half) for below, half in zip(belows, halves)]
        ys = [split(merge_rows(jnp.zeros((n, n), F32), y, size)) for y in ys]
        zs = [
            both_split(odd_rows(mh, size), odd_rows(ml, size), *y)
            for (mh, ml), y in zip(halves, ys)
        ]
        ms = [merge_rows(m, odd_rows(m, size) - z, size) for m, z in zip(ms, zs)]
        size *= 2
    return ms


def block_factors(blocks):
    n, width = blocks[0][1].shape
    tokens = blocks[0][0].shape[0]
    row = lax.broadcasted_iota(jnp.int32, (n, n), 0)
    col = lax.broadcasted_iota(jnp.int32, (n, n), 1)
    trow = lax.broadcasted_iota(jnp.int32, (tokens, n), 0)
    tcol = lax.broadcasted_iota(jnp.int32, (tokens, n), 1)
    visible = tcol < (trow + 1) * (n // tokens)
    kqs = [cat([k, q], 0) for q, k, _ in blocks]
    products = [mm(kq, k, ((1,), (1,))) for kq, (_, k, _) in zip(kqs, blocks)]
    xs, d_cols, d_rows, seens = [], [], [], []
    for gs in products:
        gram = gs[:n]
        diag = jnp.where(row == col, gram, 0.0)
        d_col = lax.rsqrt(jnp.sum(diag, axis=1, keepdims=True) + 1e-06)
        d_row = lax.rsqrt(jnp.sum(diag, axis=0, keepdims=True) + 1e-06)
        xs.append(jnp.where(col < row, (2.0 * d_col) * gram * d_row, 0.0))
        d_cols.append(d_col)
        d_rows.append(d_row)
        seens.append(split(jnp.where(visible, gs[n:], 0.0)))
    scaled = [m * (2.0 * d_col) for m, d_col in zip(unit_lower_inverses(xs), d_cols)]
    feds = [exact_right(m, v) for m, (_, _, v) in zip(scaled, blocks)]
    nears = [split(m * d_row) for m, d_row in zip(scaled, d_rows)]
    return kqs, nears, feds, seens


def local_maps(q_ref, k_ref, v_ref, local_ref, gain_ref, first, picked):
    tokens, _, width = q_ref.shape
    heads = len(picked)
    per_token = k_ref.shape[2]
    step = min(BLOCK, tokens)
    n = step * per_token
    count = tokens // step
    blocks = [
        (
            q_ref[b * step : (b + 1) * step, h],
            k_ref[b * step : (b + 1) * step, h].reshape(n, width),
            v_ref[b * step : (b + 1) * step, h].reshape(n, width),
        )
        for b in range(count)
        for h in picked
    ]
    kqs, nears, feds, seens = block_factors(blocks)
    row = lax.broadcasted_iota(jnp.int32, (width, width), 0)
    col = lax.broadcasted_iota(jnp.int32, (width, width), 1)
    eye = jnp.where(row == col, 1.0, 0.0)
    pairs = [cat([jnp.zeros((width, width), F32), eye], 1)] * heads
    for b in range(count):
        at = slice(b * heads, (b + 1) * heads)
        if b == 0:
            qs = [kq[n:].astype(F32) for kq in kqs[at]]
            passed = [cat([jnp.zeros_like(q), q], 1) for q in qs]
            feeds = [
                cat([fed, -mm(cat(list(near), 1), cat([kq[:n], kq[:n]], 0))], 1)
                for fed, near, kq in zip(feds[at], nears[at], kqs[at])
            ]
        else:
            aheads = [exact_left(kq, pair) for kq, pair in zip(kqs[at], pairs)]
            passed = [ahead[n:] for ahead in aheads]
            feeds = [
                cat([fed, jnp.zeros_like(fed)], 1) - both_split(*near, *split(ahead[:n]))
                for fed, near, ahead in zip(feds[at], nears[at], aheads)
            ]
        feeds = [split(feed) for feed in feeds]
        pairs = [
            pair + mm(cat([kq[:n], kq[:n]], 0), cat(list(feed), 0), ((0,), (0,)))
            for pair, kq, feed in zip(pairs, kqs[at], feeds)
        ]
        outs = [
            base + both_split(*seen, *feed)
            for base, seen, feed in zip(passed, seens[at], feeds)
        ]
        for h, out in zip(picked, outs):
            local_ref[first + h, b * step : (b + 1) * step] = out[:, :width]
            gain_ref[first + h, b * step : (b + 1) * step] = out[:, width:]
    return pairs


def landed(ref, at, sem):
    pltpu.make_async_copy(ref.at[at], ref.at[at], sem.at[at]).wait()


def mixer_kernel(
    ns,
    nh,
    q_ref,
    k_ref,
    v_ref,
    init_ref,
    out_ref,
    local,
    gain,
    t_own,
    a_own,
    t_box,
    a_box,
    t_out,
    a_out,
    t_line,
    a_line,
    s_line,
    s_in,
    s_fwd,
    init_box,
    t_send,
    a_send,
    t_recv,
    a_recv,
    tl_recv,
    al_recv,
    sl_send,
    s_send,
    s_recv,
    i_send,
    i_recv,
):
    size, width = q_ref.shape[1], q_ref.shape[2]
    heads = out_ref.shape[0]
    step = pl.program_id(0)
    s, z = lax.axis_index("seq"), lax.axis_index("head")
    n = ns * nh
    me = s * nh + z
    way = UNIT // 2
    ticks = heads // UNIT
    ends = (0, nh - 1)
    at_end = (z == 0) | (z == nh - 1)

    def place(p):
        return p // nh, lax.rem(p, nh)

    def head_of(group, up, j):
        return group * UNIT + up * way + j

    def slot_of(group, j):
        index = group * way + j
        return lax.rem(index, ns), index // ns

    def remote(src, dst, send, recv, where):
        return pltpu.make_async_remote_copy(
            src_ref=src,
            dst_ref=dst,
            send_sem=send,
            recv_sem=recv,
            device_id=where,
            device_id_type=MESH,
        )

    def hop(h, up, t_src, a_src):
        where = (s, z + 1 if up else z - 1)
        return [
            remote(t_src.at[h], t_box.at[h], t_send.at[h], t_recv.at[h], where),
            remote(a_src.at[h], a_box.at[h], a_send.at[h], a_recv.at[h], where),
        ]

    def to_owner(h, owner, slot):
        where = (owner, z)
        return [
            remote(
                t_out.at[h], t_line.at[slot, s], t_send.at[h], tl_recv.at[slot, s], where
            ),
            remote(
                a_out.at[h], a_line.at[slot, s], a_send.at[h], al_recv.at[slot, s], where
            ),
        ]

    def from_owner(h, slot, line):
        return remote(
            s_line.at[slot, line], s_in.at[h], sl_send.at[slot, line], s_recv.at[h], (line, z)
        )

    def state_hop(h, up, src):
        where = (s, z - 1 if up else z + 1)
        return remote(src.at[h], s_in.at[h], s_send.at[h], s_recv.at[h], where)

    def place_of(up):
        return z if up else nh - 1 - z

    def compose(tick, up):
        spot = place_of(up)
        group = tick - spot

        @pl.when((spot > 0) & (group >= 0) & (group < ticks))
        def _():
            picked = [head_of(group, up, j) for j in range(way)]
            for h in picked:
                landed(t_box, h, t_recv)
                landed(a_box, h, a_recv)

            @pl.when((spot < nh - 1) | (s < ns - 1))
            def _():
                for h in picked:
                    if up:
                        both_maps = cat([t_box[h], a_box[h].astype(F32)], 1)
                        made = both(t_own[h], both_maps)
                        extra = a_own[h]
                    else:
                        both_maps = cat([t_own[h], a_own[h].astype(F32)], 1)
                        made = both(t_box[h], both_maps)
                        extra = a_box[h]
                    t_out[h] = made[:, :width]
                    a_out[h] = (made[:, width:] + extra.astype(F32)).astype(a_out.dtype)

                @pl.when(spot < nh - 1)
                def _():
                    for h in picked:
                        for copy in hop(h, up, t_out, a_out):
                            copy.start()

                @pl.when(spot == nh - 1)
                def _():
                    for j, h in enumerate(picked):
                        owner, slot = slot_of(group, j)

                        @pl.when(owner != s)
                        def _():
                            for copy in to_owner(h, owner, slot):
                                copy.start()

                        @pl.when(owner == s)
                        def _():
                            pltpu.make_async_copy(
                                t_out.at[h], t_line.at[slot, s], tl_recv.at[slot, s]
                            ).start()
                            pltpu.make_async_copy(
                                a_out.at[h], a_line.at[slot, s], al_recv.at[slot, s]
                            ).start()

    def chain(tick):
        group = tick - nh
        j = lax.rem(s + ns * ticks * way - group * way, ns)

        @pl.when(at_end & (group >= 0) & (group < ticks) & (j < way))
        def _():
            slot = (group * way + j) // ns
            h = group * UNIT + jnp.where(z == 0, 0, way) + j
            landed(init_box, slot, i_recv)

            def send(line, state):
                s_line[slot, line] = state.astype(s_line.dtype)

                @pl.when(line != s)
                def _():
                    from_owner(h, slot, line).start()

                @pl.when(line == s)
                def _():
                    pltpu.make_async_copy(
                        s_line.at[slot, line], s_in.at[h], s_recv.at[h]
                    ).start()

            def advance(line, state):
                send(line, state)
                landed(t_line, (slot, line), tl_recv)
                landed(a_line, (slot, line), al_recv)
                return both(t_line[slot, line], state) + a_line[slot, line].astype(F32)

            send(ns - 1, lax.fori_loop(0, ns - 1, advance, init_box[slot]))

    def finish(h, state):
        raw = local[h] + exact_right(gain[h], state)
        mean = jnp.mean(raw * raw, axis=-1, keepdims=True)
        out_ref[h] = (raw * lax.rsqrt(mean + 1e-06)).astype(out_ref.dtype)

    def settle(tick, up):
        spot = place_of(up)
        group = tick - 2 * nh + spot

        @pl.when((group >= 0) & (group < ticks))
        def _():
            picked = [head_of(group, up, j) for j in range(way)]
            for h in picked:
                landed(s_in, h, s_recv)

            if up:

                @pl.when(spot > 0)
                def _():
                    for h in picked:
                        state_hop(h, up, s_in).start()
                    for h in picked:
                        state = exact_right(t_box[h], s_in[h]) + a_box[h].astype(F32)
                        finish(h, state.astype(BF16))

                @pl.when(spot == 0)
                def _():
                    for h in picked:
                        finish(h, s_in[h])

            else:

                @pl.when(spot > 0)
                def _():
                    for h in picked:
                        state = exact_right(t_own[h], s_in[h]) + a_own[h].astype(F32)
                        s_fwd[h] = state.astype(BF16)
                    for h in picked:
                        state_hop(h, up, s_fwd).start()

                for h in picked:
                    finish(h, s_in[h])

    def exchange(tick):
        for up in (0, 1):
            compose(tick, up)
        chain(tick)
        for up in (0, 1):
            settle(tick, up)

    own = init_ref.shape[0]

    def init_copies():
        for i in range(own):
            h = z * own + i
            up = (i % UNIT) // way
            owner, slot = slot_of(h // UNIT, i % way)
            copy = remote(
                init_ref.at[i], init_box.at[slot], i_send.at[i], i_recv.at[slot], (s, ends[up])
            )
            yield i, up, owner, slot, copy

    @pl.when(step == 0)
    def _():
        barrier = pltpu.get_barrier_semaphore()

        @pl.loop(1, n)
        def _(i):
            pl.semaphore_signal(
                barrier, inc=1, device_id=place(lax.rem(me + i, n)), device_id_type=MESH
            )

        pl.semaphore_wait(barrier, n - 1)

        for i, up, owner, slot, copy in init_copies():

            @pl.when((owner == s) & (z != ends[up]))
            def _():
                copy.start()

            @pl.when((owner == s) & (z == ends[up]))
            def _():
                pltpu.make_async_copy(
                    init_ref.at[i], init_box.at[slot], i_recv.at[slot]
                ).start()

    first = step * size
    for sub in range(size // UNIT):
        picked = list(range(sub * UNIT, (sub + 1) * UNIT))
        pairs = local_maps(q_ref, k_ref, v_ref, local, gain, first, picked)
        for h, pair in zip(picked, pairs):
            t_own[first + h] = pair[:, width:]
            a_own[first + h] = pair[:, :width].astype(a_own.dtype)
        for up in (0, 1):

            @pl.when(place_of(up) == 0)
            def _():
                for h in picked[up * way : (up + 1) * way]:
                    for copy in hop(first + h, up, t_own, a_own):
                        copy.start()

        exchange(step * (size // UNIT) + sub)

    @pl.when(step == pl.num_programs(0) - 1)
    def _():
        @pl.loop(ticks, ticks + 2 * nh)
        def _(tick):
            exchange(tick)

        for i, up, owner, slot, copy in init_copies():

            @pl.when((owner == s) & (z != ends[up]))
            def _():
                copy.wait_send()

        @pl.loop(0, ticks)
        def _(group):
            for up in (0, 1):
                spot = place_of(up)
                for j in range(way):
                    h = head_of(group, up, j)
                    owner, slot = slot_of(group, j)

                    @pl.when(spot < nh - 1)
                    def _():
                        for copy in hop(h, up, t_out, a_out):
                            copy.wait_send()

                    @pl.when((spot == nh - 1) & (owner != s) & (s < ns - 1))
                    def _():
                        for copy in to_owner(h, owner, slot):
                            copy.wait_send()

                    @pl.when(spot > 0)
                    def _():
                        state_hop(h, up, s_fwd).wait_send()

                    @pl.when((spot == nh - 1) & (owner == s))
                    def _():
                        @pl.loop(0, ns)
                        def _(line):
                            @pl.when(line != s)
                            def _():
                                from_owner(h, slot, line).wait_send()


def mixer(q, k, v, initial_state):
    ns, nh = lax.axis_size("seq"), lax.axis_size("head")
    tokens, heads, width = q.shape
    g = HEADS_A_STEP
    slots = heads // (2 * ns)
    dma = pltpu.SemaphoreType.DMA

    def by_token(rows):
        return pl.BlockSpec((tokens, g, rows, width), lambda i: (0, i, 0, 0))

    def maps(*lead):
        square = (*lead, width, width)
        return [pltpu.VMEM(square, F32), pltpu.VMEM(square, BF16)]

    return pl.pallas_call(
        functools.partial(mixer_kernel, ns, nh),
        grid=(heads // g,),
        in_specs=[
            pl.BlockSpec((tokens, g, width), lambda i: (0, i, 0)),
            by_token(k.shape[2]),
            by_token(k.shape[2]),
            pl.BlockSpec(initial_state.shape, lambda i: (0, 0, 0)),
        ],
        out_specs=pl.BlockSpec((heads, tokens, width), lambda i: (0, 0, 0)),
        out_shape=jax.ShapeDtypeStruct((heads, tokens, width), BF16),
        scratch_shapes=[
            pltpu.VMEM((heads, tokens, width), F32),
            pltpu.VMEM((heads, tokens, width), F32),
            *maps(heads),
            *maps(heads),
            *maps(heads),
            *maps(slots, ns),
            pltpu.VMEM((slots, ns, width, width), BF16),
            pltpu.VMEM((heads, width, width), BF16),
            pltpu.VMEM((heads, width, width), BF16),
            pltpu.VMEM((slots, width, width), F32),
            dma((heads,)),
            dma((heads,)),
            dma((heads,)),
            dma((heads,)),
            dma((slots, ns)),
            dma((slots, ns)),
            dma((slots, ns)),
            dma((heads,)),
            dma((heads,)),
            dma((initial_state.shape[0],)),
            dma((slots,)),
        ],
        compiler_params=pltpu.CompilerParams(
            collective_id=0, has_side_effects=True, vmem_limit_bytes=VMEM_BYTES
        ),
        name="mixer",
    )(q, k, v, initial_state)


def owned_per_device(queries, keys, values, initial_state):
    tokens, heads, width = queries.shape
    return jnp.swapaxes(mixer(queries, keys, values, initial_state), 0, 1)


HIGH = lax.Precision.HIGHEST


def shifted(value, axis, by):
    size = lax.axis_size(axis)
    pairs = [(i, i + by) for i in range(size) if 0 <= i + by < size]
    return lax.ppermute(value, axis, pairs)


def matmul(left, right):
    return jnp.dot(left, right, precision=HIGH, preferred_element_type=jnp.float32)


def batched(left, right):
    return jnp.einsum("hij,hjk->hik", left, right, precision=HIGH)


def unit_rows(raw_keys):
    floats = raw_keys.astype(jnp.float32)
    return floats * lax.rsqrt(jnp.sum(floats * floats, axis=-1, keepdims=True) + 1e-06)


def all_factors(k_blocks, v_blocks):
    updates = k_blocks.shape[2]
    head_width = k_blocks.shape[3]
    gram = jnp.einsum("hbid,hbjd->hbij", k_blocks, k_blocks, precision=HIGH)
    system = jnp.eye(updates, dtype=jnp.float32) + jnp.tril(2.0 * gram, -1)
    solved = lax.linalg.triangular_solve(
        system,
        2.0 * jnp.concatenate([k_blocks, v_blocks], axis=-1),
        left_side=True,
        lower=True,
        unit_diagonal=True,
    )
    return (solved[..., :head_width], solved[..., head_width:])


def visible_scores(q_blk, k_blk):
    rows = q_blk.shape[0]
    updates = k_blk.shape[0]
    per_token = updates // rows
    row_ids = lax.broadcasted_iota(jnp.int32, (rows, updates), 0)
    col_ids = lax.broadcasted_iota(jnp.int32, (rows, updates), 1)
    return jnp.where(col_ids < (row_ids + 1) * per_token, matmul(q_blk, k_blk.T), 0.0)


def start_pair(head_width):
    return jnp.concatenate(
        [jnp.zeros((head_width, head_width), jnp.float32), jnp.eye(head_width, dtype=jnp.float32)],
        axis=1,
    )


def carried_pass(q_blocks, k_blocks, w_blocks, u_blocks):
    head_width = q_blocks.shape[2]

    def advance(pair_state, block_item):
        q_blk, k_blk, w_mat, u_mat = block_item
        feed_rows = jnp.concatenate([u_mat, jnp.zeros_like(u_mat)], axis=1) - matmul(
            w_mat, pair_state
        )
        outputs = matmul(q_blk, pair_state) + matmul(visible_scores(q_blk, k_blk), feed_rows)
        return (pair_state + matmul(k_blk.T, feed_rows), outputs)

    final_pair, outputs = lax.scan(
        advance, start_pair(head_width), (q_blocks, k_blocks, w_blocks, u_blocks)
    )
    outputs = outputs.reshape(-1, 2 * head_width)
    return (
        final_pair[:, head_width:],
        final_pair[:, :head_width],
        outputs[:, :head_width],
        outputs[:, head_width:],
    )


def per_device(queries, keys, values, initial_state):
    q_heads, k_heads, v_heads = (
        lax.all_to_all(queries, "head", split_axis=1, concat_axis=0, tiled=True),
        lax.all_to_all(keys, "head", split_axis=1, concat_axis=0, tiled=True),
        lax.all_to_all(values, "head", split_axis=1, concat_axis=0, tiled=True),
    )
    head_width = q_heads.shape[2]
    local_heads = q_heads.shape[1]
    blocks = q_heads.shape[0] // BLOCK
    q_blocks = jnp.moveaxis(q_heads.astype(jnp.float32), 1, 0).reshape(
        local_heads, blocks, BLOCK, head_width
    )
    k_blocks = jnp.moveaxis(unit_rows(k_heads), 1, 0).reshape(local_heads, blocks, -1, head_width)
    v_blocks = jnp.moveaxis(v_heads.astype(jnp.float32), 1, 0).reshape(
        local_heads, blocks, -1, head_width
    )
    w_blocks, u_blocks = all_factors(k_blocks, v_blocks)
    transition, additive, local_out, query_gain = jax.vmap(carried_pass)(
        q_blocks, k_blocks, w_blocks, u_blocks
    )
    at_first = lax.axis_index("seq") == 0
    start_state = jnp.where(at_first, initial_state, jnp.zeros_like(initial_state))

    def relay_step(loop_step, current):
        passed = shifted(batched(transition, current) + additive, "seq", 1)
        return jnp.where(at_first, initial_state, passed)

    incoming = lax.fori_loop(0, lax.axis_size("seq") - 1, relay_step, start_state)
    raw_out = local_out + batched(query_gain, incoming)
    scaled = raw_out * lax.rsqrt(jnp.mean(raw_out * raw_out, axis=-1, keepdims=True) + 1e-06)
    tokens_major = jnp.moveaxis(scaled.astype(jnp.bfloat16), 0, 1)
    return lax.all_to_all(tokens_major, "head", split_axis=0, concat_axis=1, tiled=True)


def solution(mesh):
    placed = (
        P(("seq", "head"), None, None),
        P(("seq", "head"), None, None, None),
        P(("seq", "head"), None, None, None),
        P("head", None, None),
    )

    def chosen(queries, keys, values, initial_state):
        own_heads = initial_state.shape[0]
        ns, nh = mesh.shape["seq"], mesh.shape["head"]
        fits = own_heads % HEADS_A_STEP == 0 and own_heads * nh % (2 * ns) == 0
        if fits and nh > 1:
            return owned_per_device(queries, keys, values, initial_state)
        return per_device(queries, keys, values, initial_state)

    return jax.shard_map(
        chosen,
        mesh=mesh,
        in_specs=placed,
        out_specs=P(("seq", "head"), None, None),
        check_vma=False,
    )
```

```python
import functools
import itertools

import jax
import jax.numpy as jnp
from jax import lax
from jax.experimental import pallas as pl
from jax.experimental.pallas import tpu as pltpu
from jax.sharding import PartitionSpec as P

BLOCK = 64
BASE = 16
HEADS_A_STEP = 8
UNIT = 4
GROUP = 4
GRAM_SHARE = 0.25
BASE_SHARE = 1.15
VMEM_BYTES = 56 << 20

F32 = jnp.float32
BF16 = jnp.bfloat16
MESH = pl.DeviceIdType.MESH


def mm(left, right, dims=((1,), (0,))):
    return lax.dot_general(left, right, (dims, ((), ())), preferred_element_type=F32)


def split(x):
    high = x.astype(BF16)
    return high, (x - high.astype(F32)).astype(BF16)


def cat(parts, axis):
    return jnp.concatenate(parts, axis=axis)


def exact_left(left, right):
    high, low = split(right)
    return mm(cat([left, left], 1), cat([high, low], 0))


def exact_right(left, right):
    high, low = split(left)
    return mm(cat([high, low], 1), cat([right, right], 0))


def both_split(lh, ll, rh, rl):
    return mm(cat([lh, ll], 1), cat([rh, rh], 0)) + mm(lh, rl)


def both(left, right):
    return both_split(*split(left), *split(right))


def odd_rows(x, size):
    rows = x.shape[0]
    return cat([x[s : s + size] for s in range(size, rows, 2 * size)], 0)


def merge_rows(even_from, odd, size):
    rows = even_from.shape[0]
    parts = []
    for i, s in enumerate(range(0, rows, 2 * size)):
        parts += [even_from[s : s + size], odd[i * size : (i + 1) * size]]
    return cat(parts, 0)


def twice(pair, right_high, right_low):
    k = right_high.shape[0]
    return mm(pair, cat([right_high, right_high], 0)) + mm(pair[:, :k], right_low)


def grams(q_ref, k_ref, v_ref, picked, kq_ref, v_own, x_ref, m_ref, d_ref, seen_ref):
    tokens, _, width = q_ref.shape
    per_token = k_ref.shape[2]
    step = min(BLOCK, tokens)
    n = step * per_token
    row = lax.broadcasted_iota(jnp.int32, (n, n), 0)
    col = lax.broadcasted_iota(jnp.int32, (n, n), 1)
    trow = lax.broadcasted_iota(jnp.int32, (step, n), 0)
    tcol = lax.broadcasted_iota(jnp.int32, (step, n), 1)
    visible = tcol < (trow + 1) * per_token
    for b in range(tokens // step):
        for j, h in enumerate(picked):
            i = b * len(picked) + j
            here = slice(b * step, (b + 1) * step)
            k = k_ref[here, h].reshape(n, width)
            kq = cat([k, q_ref[here, h]], 0)
            kq_ref[i] = kq
            v_own[i] = v_ref[here, h].reshape(n, width)
            gs = mm(kq, k, ((1,), (1,)))
            gram = gs[:n]
            diag = jnp.where(row == col, gram, 0.0)
            norm = jnp.sum(diag, axis=1, keepdims=True) + 1e-06
            d_ref[i] = lax.rsqrt(jnp.sum(diag, axis=0, keepdims=True) + 1e-06)
            d_col = lax.rsqrt(norm)
            x = jnp.where(col < row, (2.0 * d_col * d_col) * gram, 0.0)
            x_ref[i] = cat(split(x), 1)
            seen_ref[i] = cat(split(jnp.where(visible, gs[n:], 0.0)), 1)
            packed = jnp.where(col[:BASE] < BASE, x[:BASE], 0.0)
            for s in range(BASE, n, BASE):
                inside = (col[:BASE] >= s) & (col[:BASE] < s + BASE)
                packed = jnp.where(inside, x[s : s + BASE], packed)
            m_ref[i] = packed
            yield


def base_inverses(m_ref):
    blocks, _, n = m_ref.shape
    sub = lax.broadcasted_iota(jnp.int32, (BASE, n), 0)
    lane = lax.broadcasted_iota(jnp.int32, (BASE, n), 1)
    invs = [jnp.where(sub == lane % BASE, 1.0, 0.0)] * blocks
    for j in range(BASE - 1):
        at = lane - lane % BASE + j
        for i in range(blocks):
            coef = jnp.take_along_axis(m_ref[i], at, axis=1)
            invs[i] = invs[i] - coef * invs[i][j : j + 1]
            if i % GROUP == GROUP - 1:
                yield
    for i, inv in enumerate(invs):
        m_ref[i] = inv


def inverses(v_own, x_ref, m_ref, d_ref, near_ref, fed_ref):
    blocks, n, _ = near_ref.shape
    row = lax.broadcasted_iota(jnp.int32, (n, n), 0)
    col = lax.broadcasted_iota(jnp.int32, (n, n), 1)
    same = row // BASE == col // BASE
    every = range(blocks)
    ms = [jnp.where(same, cat([m_ref[i]] * (n // BASE), 0), 0.0) for i in every]
    size = BASE
    while size < n:
        near = odd_rows(col // size - row // size, size) == -1
        halves, ys = [], []
        for i in every:
            halves.append(split(ms[i]))
            ys.append(twice(odd_rows(x_ref[i], size), *halves[i]))
            if i % GROUP == GROUP - 1:
                yield
        for i in every:
            y = jnp.where(near, ys[i], 0.0)
            ys[i] = split(merge_rows(jnp.zeros((n, n), F32), y, size))
            if i % GROUP == GROUP - 1:
                yield
        for i in every:
            mh, ml = halves[i]
            z = both_split(odd_rows(mh, size), odd_rows(ml, size), *ys[i])
            ms[i] = merge_rows(ms[i], odd_rows(ms[i], size) - z, size)
            if i % GROUP == GROUP - 1:
                yield
        size *= 2
    for i in every:
        d = d_ref[i]
        fed_ref[i] = exact_right(ms[i] * (2.0 * d), v_own[i])
        near_ref[i] = cat(split(ms[i] * (2.0 * d * d)), 1)
        if i % GROUP == GROUP - 1:
            yield


def local_maps(
    heads, kq_ref, near_ref, fed_ref, seen_ref, local_ref, gain_ref, t_ref, a_ref, first
):
    _, rows, width = kq_ref.shape
    n = near_ref.shape[1]
    step = rows - n
    count = kq_ref.shape[0] // heads
    row = lax.broadcasted_iota(jnp.int32, (width, width), 0)
    col = lax.broadcasted_iota(jnp.int32, (width, width), 1)
    eye = jnp.where(row == col, 1.0, 0.0)
    pairs = [cat([jnp.zeros((width, width), F32), eye], 1)] * heads
    for b in range(count):
        at = range(b * heads, (b + 1) * heads)
        if b == 0:
            passed, feeds = [], []
            for i in at:
                kq = kq_ref[i]
                q = kq[n:].astype(F32)
                passed.append(cat([jnp.zeros_like(q), q], 1))
                feeds.append(cat([fed_ref[i], -mm(near_ref[i], cat([kq[:n], kq[:n]], 0))], 1))
                yield
        else:
            aheads = []
            for i, pair in zip(at, pairs):
                aheads.append(exact_left(kq_ref[i], pair))
                yield
            passed = [ahead[n:] for ahead in aheads]
            feeds = []
            for i, ahead in zip(at, aheads):
                fed = cat([fed_ref[i], jnp.zeros((n, width), F32)], 1)
                feeds.append(fed - twice(near_ref[i], *split(ahead[:n])))
                yield
        feeds = [split(feed) for feed in feeds]
        made = []
        for i, pair, feed in zip(at, pairs, feeds):
            k = kq_ref[i, :n]
            made.append(pair + mm(cat([k, k], 0), cat(list(feed), 0), ((0,), (0,))))
            yield
        pairs = made
        for h, (i, base, feed) in enumerate(zip(at, passed, feeds)):
            out = base + twice(seen_ref[i], *feed)
            local_ref[first + h, b * step : (b + 1) * step] = out[:, :width]
            gain_ref[first + h, b * step : (b + 1) * step] = out[:, width:]
            yield
    for h, pair in enumerate(pairs):
        t_ref[first + h] = pair[:, width:]
        a_ref[first + h] = pair[:, :width].astype(a_ref.dtype)


def weave(mains, sides, share):
    owed = 0.0
    for _ in mains:
        owed += share
        while owed >= 1.0:
            owed -= 1.0
            next(sides, None)


def landed(ref, at, sem):
    pltpu.make_async_copy(ref.at[at], ref.at[at], sem.at[at]).wait()


def mixer_kernel(
    ns,
    nh,
    q_ref,
    k_ref,
    v_ref,
    init_ref,
    out_ref,
    local,
    gain,
    t_own,
    a_own,
    t_box,
    a_box,
    t_out,
    a_out,
    t_line,
    a_line,
    s_line,
    s_in,
    s_fwd,
    init_box,
    t_send,
    a_send,
    t_recv,
    a_recv,
    tl_recv,
    al_recv,
    sl_send,
    s_send,
    s_recv,
    i_send,
    i_recv,
    *stages,
):
    size, width = q_ref.shape[1], q_ref.shape[2]
    heads = out_ref.shape[0]
    step = pl.program_id(0)
    s, z = lax.axis_index("seq"), lax.axis_index("head")
    n = ns * nh
    me = s * nh + z
    way = UNIT // 2
    ticks = heads // UNIT
    ends = (0, nh - 1)
    at_end = (z == 0) | (z == nh - 1)

    def place(p):
        return p // nh, lax.rem(p, nh)

    def head_of(group, up, j):
        return group * UNIT + up * way + j

    def slot_of(group, j):
        index = group * way + j
        turn = lax.rem(index, ns)
        half = turn // 2
        return jnp.where(lax.rem(turn, 2) == 0, half, ns - 1 - half), index // ns

    def remote(src, dst, send, recv, where):
        return pltpu.make_async_remote_copy(
            src_ref=src,
            dst_ref=dst,
            send_sem=send,
            recv_sem=recv,
            device_id=where,
            device_id_type=MESH,
        )

    def hop(h, up, t_src, a_src):
        where = (s, z + 1 if up else z - 1)
        return [
            remote(t_src.at[h], t_box.at[h], t_send.at[h], t_recv.at[h], where),
            remote(a_src.at[h], a_box.at[h], a_send.at[h], a_recv.at[h], where),
        ]

    def to_owner(h, owner, slot):
        where = (owner, z)
        return [
            remote(
                t_out.at[h], t_line.at[slot, s], t_send.at[h], tl_recv.at[slot, s], where
            ),
            remote(
                a_out.at[h], a_line.at[slot, s], a_send.at[h], al_recv.at[slot, s], where
            ),
        ]

    def from_owner(h, slot, line):
        return remote(
            s_line.at[slot, line], s_in.at[h], sl_send.at[slot, line], s_recv.at[h], (line, z)
        )

    def state_hop(h, up, src):
        where = (s, z - 1 if up else z + 1)
        return remote(src.at[h], s_in.at[h], s_send.at[h], s_recv.at[h], where)

    def place_of(up):
        return z if up else nh - 1 - z

    def compose(tick, up):
        spot = place_of(up)
        group = tick - spot

        @pl.when((spot > 0) & (group >= 0) & (group < ticks))
        def _():
            for j in range(way):
                join(group, up, j, spot)

    def join(group, up, j, spot):
        h = head_of(group, up, j)
        landed(t_box, h, t_recv)
        landed(a_box, h, a_recv)

        @pl.when((spot < nh - 1) | (s < ns - 1))
        def _():
            if up:
                later_t, later_a, sooner_t, sooner_a = t_own, a_own, t_box, a_box
            else:
                later_t, later_a, sooner_t, sooner_a = t_box, a_box, t_own, a_own
            made = both(later_t[h], cat([sooner_t[h], sooner_a[h].astype(F32)], 1))
            t_out[h] = made[:, :width]
            a_out[h] = (made[:, width:] + later_a[h].astype(F32)).astype(a_out.dtype)

            @pl.when(spot < nh - 1)
            def _():
                for copy in hop(h, up, t_out, a_out):
                    copy.start()

            owner, slot = slot_of(group, j)

            @pl.when((spot == nh - 1) & (owner != s))
            def _():
                for copy in to_owner(h, owner, slot):
                    copy.start()

            @pl.when((spot == nh - 1) & (owner == s))
            def _():
                pltpu.make_async_copy(
                    t_out.at[h], t_line.at[slot, s], tl_recv.at[slot, s]
                ).start()
                pltpu.make_async_copy(
                    a_out.at[h], a_line.at[slot, s], al_recv.at[slot, s]
                ).start()

    def chain(tick):
        group = tick - nh
        turn = jnp.where(s < ns // 2, 2 * s, 2 * (ns - 1 - s) + 1)
        j = lax.rem(turn + ns * ticks * way - group * way, ns)

        @pl.when(at_end & (group >= 0) & (group < ticks) & (j < way))
        def _():
            slot = (group * way + j) // ns
            h = group * UNIT + jnp.where(z == 0, 0, way) + j
            landed(init_box, slot, i_recv)

            def send(line, state):
                s_line[slot, line] = state.astype(s_line.dtype)

                @pl.when(line != s)
                def _():
                    from_owner(h, slot, line).start()

                @pl.when(line == s)
                def _():
                    pltpu.make_async_copy(
                        s_line.at[slot, line], s_in.at[h], s_recv.at[h]
                    ).start()

            def advance(line, state):
                send(line, state)
                landed(t_line, (slot, line), tl_recv)
                landed(a_line, (slot, line), al_recv)
                return both(t_line[slot, line], state) + a_line[slot, line].astype(F32)

            send(ns - 1, lax.fori_loop(0, ns - 1, advance, init_box[slot], unroll=True))

    def finish(h, read):
        raw = local[h] + read
        mean = jnp.mean(raw * raw, axis=-1, keepdims=True)
        out_ref[h] = (raw * lax.rsqrt(mean + 1e-06)).astype(out_ref.dtype)

    def settle(tick, up):
        spot = place_of(up)
        group = tick - 2 * nh + spot

        @pl.when((group >= 0) & (group < ticks))
        def _():
            picked = [head_of(group, up, j) for j in range(way)]
            if up:

                @pl.when(spot > 0)
                def _():
                    for h in picked:
                        landed(s_in, h, s_recv)
                        state_hop(h, up, s_in).start()
                    for h in picked:
                        state = exact_right(t_box[h], s_in[h]) + a_box[h].astype(F32)
                        finish(h, both(gain[h], state))

                @pl.when(spot == 0)
                def _():
                    for h in picked:
                        landed(s_in, h, s_recv)
                    for h in picked:
                        finish(h, exact_right(gain[h], s_in[h]))

            else:
                for h in picked:
                    landed(s_in, h, s_recv)

                @pl.when(spot > 0)
                def _():
                    for h in picked:
                        state = exact_right(t_own[h], s_in[h]) + a_own[h].astype(F32)
                        s_fwd[h] = state.astype(BF16)
                        state_hop(h, up, s_fwd).start()

                for h in picked:
                    finish(h, exact_right(gain[h], s_in[h]))

    def exchange(tick):
        for up in (0, 1):
            compose(tick, up)
        chain(tick)
        for up in (0, 1):
            settle(tick, up)

    own = init_ref.shape[0]

    def init_copies():
        for i in range(own):
            h = z * own + i
            up = (i % UNIT) // way
            owner, slot = slot_of(h // UNIT, i % way)
            copy = remote(
                init_ref.at[i], init_box.at[slot], i_send.at[i], i_recv.at[slot], (s, ends[up])
            )
            yield i, up, owner, slot, copy

    @pl.when(step == 0)
    def _():
        barrier = pltpu.get_barrier_semaphore()

        @pl.loop(1, n)
        def _(i):
            pl.semaphore_signal(
                barrier, inc=1, device_id=place(lax.rem(me + i, n)), device_id_type=MESH
            )

    subs = size // UNIT
    kept = len(stages) // subs

    def stage_of(sub):
        return stages[sub * kept : (sub + 1) * kept]

    def picked_of(sub):
        return list(range(sub * UNIT, (sub + 1) * UNIT))

    def advance_maps(done, first, later):
        none = iter(())
        invert, carry, gram, base = none, none, none, none
        if done is not None:
            kq, near, fed, seen, v_own, x, m, d = stage_of(done)
            invert = inverses(v_own, x, m, d, near, fed)
            carry = local_maps(
                UNIT, kq, near, fed, seen, local, gain, t_own, a_own, first
            )
        if later is not None:
            kq, near, fed, seen, v_own, x, m, d = stage_of(later)
            gram = grams(
                q_ref, k_ref, v_ref, picked_of(later), kq, v_own, x, m, d, seen
            )
            base = base_inverses(m)
        sides = itertools.chain(gram, base)
        weave(invert, sides, GRAM_SHARE)
        weave(carry, sides, BASE_SHARE)
        for _ in sides:
            pass

    def offer(first):
        for up in (0, 1):

            @pl.when(place_of(up) == 0)
            def _():
                for j in range(way):
                    for copy in hop(first + up * way + j, up, t_own, a_own):
                        copy.start()

    @pl.when(step == 0)
    def _():
        advance_maps(None, None, 0)
        pl.semaphore_wait(pltpu.get_barrier_semaphore(), n - 1)
        for i, up, owner, slot, copy in init_copies():

            @pl.when((owner == s) & (z != ends[up]))
            def _():
                copy.start()

            @pl.when((owner == s) & (z == ends[up]))
            def _():
                pltpu.make_async_copy(
                    init_ref.at[i], init_box.at[slot], i_recv.at[slot]
                ).start()

    @pl.when(step > 0)
    def _():
        advance_maps(subs - 1, step * size - UNIT, 0)
        offer(step * size - UNIT)
        exchange(step * subs - 1)

    for sub in range(1, subs):
        advance_maps(sub - 1, step * size + (sub - 1) * UNIT, sub)
        offer(step * size + (sub - 1) * UNIT)
        exchange(step * subs + sub - 1)

    @pl.when(step == pl.num_programs(0) - 1)
    def _():
        advance_maps(subs - 1, heads - UNIT, None)
        offer(heads - UNIT)

        @pl.loop(ticks - 1, ticks + 2 * nh)
        def _(tick):
            exchange(tick)

        for i, up, owner, slot, copy in init_copies():

            @pl.when((owner == s) & (z != ends[up]))
            def _():
                copy.wait_send()

        @pl.loop(0, ticks)
        def _(group):
            for up in (0, 1):
                spot = place_of(up)
                for j in range(way):
                    h = head_of(group, up, j)
                    owner, slot = slot_of(group, j)

                    @pl.when(spot < nh - 1)
                    def _():
                        for copy in hop(h, up, t_out, a_out):
                            copy.wait_send()

                    @pl.when((spot == nh - 1) & (owner != s) & (s < ns - 1))
                    def _():
                        for copy in to_owner(h, owner, slot):
                            copy.wait_send()

                    @pl.when(spot > 0)
                    def _():
                        state_hop(h, up, s_fwd).wait_send()

                    @pl.when((spot == nh - 1) & (owner == s))
                    def _():
                        @pl.loop(0, ns)
                        def _(line):
                            @pl.when(line != s)
                            def _():
                                from_owner(h, slot, line).wait_send()


def mixer(q, k, v, initial_state):
    ns, nh = lax.axis_size("seq"), lax.axis_size("head")
    tokens, heads, width = q.shape
    g = HEADS_A_STEP
    slots = heads // (2 * ns)
    dma = pltpu.SemaphoreType.DMA

    def by_token(rows):
        return pl.BlockSpec((tokens, g, rows, width), lambda i: (0, i, 0, 0))

    def maps(*lead):
        square = (*lead, width, width)
        return [pltpu.VMEM(square, F32), pltpu.VMEM(square, BF16)]

    step = min(BLOCK, tokens)
    n = step * k.shape[2]
    blocks = UNIT * (tokens // step)
    stage = [
        pltpu.VMEM((blocks, n + step, width), BF16),
        pltpu.VMEM((blocks, n, 2 * n), BF16),
        pltpu.VMEM((blocks, n, width), F32),
        pltpu.VMEM((blocks, step, 2 * n), BF16),
        pltpu.VMEM((blocks, n, width), BF16),
        pltpu.VMEM((blocks, n, 2 * n), BF16),
        pltpu.VMEM((blocks, BASE, n), F32),
        pltpu.VMEM((blocks, 1, n), F32),
    ]
    return pl.pallas_call(
        functools.partial(mixer_kernel, ns, nh),
        grid=(heads // g,),
        in_specs=[
            pl.BlockSpec((tokens, g, width), lambda i: (0, i, 0)),
            by_token(k.shape[2]),
            by_token(k.shape[2]),
            pl.BlockSpec(initial_state.shape, lambda i: (0, 0, 0)),
        ],
        out_specs=pl.BlockSpec((heads, tokens, width), lambda i: (0, 0, 0)),
        out_shape=jax.ShapeDtypeStruct((heads, tokens, width), BF16),
        scratch_shapes=[
            pltpu.VMEM((heads, tokens, width), F32),
            pltpu.VMEM((heads, tokens, width), F32),
            *maps(heads),
            *maps(heads),
            *maps(heads),
            *maps(slots, ns),
            pltpu.VMEM((slots, ns, width, width), BF16),
            pltpu.VMEM((heads, width, width), BF16),
            pltpu.VMEM((heads, width, width), BF16),
            pltpu.VMEM((slots, width, width), F32),
            dma((heads,)),
            dma((heads,)),
            dma((heads,)),
            dma((heads,)),
            dma((slots, ns)),
            dma((slots, ns)),
            dma((slots, ns)),
            dma((heads,)),
            dma((heads,)),
            dma((initial_state.shape[0],)),
            dma((slots,)),
            *stage * (g // UNIT),
        ],
        compiler_params=pltpu.CompilerParams(
            collective_id=0, has_side_effects=True, vmem_limit_bytes=VMEM_BYTES
        ),
        name="mixer",
    )(q, k, v, initial_state)


def owned_per_device(queries, keys, values, initial_state):
    tokens, heads, width = queries.shape
    return jnp.swapaxes(mixer(queries, keys, values, initial_state), 0, 1)


HIGH = lax.Precision.HIGHEST


def shifted(value, axis, by):
    size = lax.axis_size(axis)
    pairs = [(i, i + by) for i in range(size) if 0 <= i + by < size]
    return lax.ppermute(value, axis, pairs)


def matmul(left, right):
    return jnp.dot(left, right, precision=HIGH, preferred_element_type=jnp.float32)


def batched(left, right):
    return jnp.einsum("hij,hjk->hik", left, right, precision=HIGH)


def unit_rows(raw_keys):
    floats = raw_keys.astype(jnp.float32)
    return floats * lax.rsqrt(jnp.sum(floats * floats, axis=-1, keepdims=True) + 1e-06)


def all_factors(k_blocks, v_blocks):
    updates = k_blocks.shape[2]
    head_width = k_blocks.shape[3]
    gram = jnp.einsum("hbid,hbjd->hbij", k_blocks, k_blocks, precision=HIGH)
    system = jnp.eye(updates, dtype=jnp.float32) + jnp.tril(2.0 * gram, -1)
    solved = lax.linalg.triangular_solve(
        system,
        2.0 * jnp.concatenate([k_blocks, v_blocks], axis=-1),
        left_side=True,
        lower=True,
        unit_diagonal=True,
    )
    return (solved[..., :head_width], solved[..., head_width:])


def visible_scores(q_blk, k_blk):
    rows = q_blk.shape[0]
    updates = k_blk.shape[0]
    per_token = updates // rows
    row_ids = lax.broadcasted_iota(jnp.int32, (rows, updates), 0)
    col_ids = lax.broadcasted_iota(jnp.int32, (rows, updates), 1)
    return jnp.where(col_ids < (row_ids + 1) * per_token, matmul(q_blk, k_blk.T), 0.0)


def start_pair(head_width):
    return jnp.concatenate(
        [jnp.zeros((head_width, head_width), jnp.float32), jnp.eye(head_width, dtype=jnp.float32)],
        axis=1,
    )


def carried_pass(q_blocks, k_blocks, w_blocks, u_blocks):
    head_width = q_blocks.shape[2]

    def advance(pair_state, block_item):
        q_blk, k_blk, w_mat, u_mat = block_item
        feed_rows = jnp.concatenate([u_mat, jnp.zeros_like(u_mat)], axis=1) - matmul(
            w_mat, pair_state
        )
        outputs = matmul(q_blk, pair_state) + matmul(visible_scores(q_blk, k_blk), feed_rows)
        return (pair_state + matmul(k_blk.T, feed_rows), outputs)

    final_pair, outputs = lax.scan(
        advance, start_pair(head_width), (q_blocks, k_blocks, w_blocks, u_blocks)
    )
    outputs = outputs.reshape(-1, 2 * head_width)
    return (
        final_pair[:, head_width:],
        final_pair[:, :head_width],
        outputs[:, :head_width],
        outputs[:, head_width:],
    )


def per_device(queries, keys, values, initial_state):
    q_heads, k_heads, v_heads = (
        lax.all_to_all(queries, "head", split_axis=1, concat_axis=0, tiled=True),
        lax.all_to_all(keys, "head", split_axis=1, concat_axis=0, tiled=True),
        lax.all_to_all(values, "head", split_axis=1, concat_axis=0, tiled=True),
    )
    head_width = q_heads.shape[2]
    local_heads = q_heads.shape[1]
    blocks = q_heads.shape[0] // BLOCK
    q_blocks = jnp.moveaxis(q_heads.astype(jnp.float32), 1, 0).reshape(
        local_heads, blocks, BLOCK, head_width
    )
    k_blocks = jnp.moveaxis(unit_rows(k_heads), 1, 0).reshape(local_heads, blocks, -1, head_width)
    v_blocks = jnp.moveaxis(v_heads.astype(jnp.float32), 1, 0).reshape(
        local_heads, blocks, -1, head_width
    )
    w_blocks, u_blocks = all_factors(k_blocks, v_blocks)
    transition, additive, local_out, query_gain = jax.vmap(carried_pass)(
        q_blocks, k_blocks, w_blocks, u_blocks
    )
    at_first = lax.axis_index("seq") == 0
    start_state = jnp.where(at_first, initial_state, jnp.zeros_like(initial_state))

    def relay_step(loop_step, current):
        passed = shifted(batched(transition, current) + additive, "seq", 1)
        return jnp.where(at_first, initial_state, passed)

    incoming = lax.fori_loop(0, lax.axis_size("seq") - 1, relay_step, start_state)
    raw_out = local_out + batched(query_gain, incoming)
    scaled = raw_out * lax.rsqrt(jnp.mean(raw_out * raw_out, axis=-1, keepdims=True) + 1e-06)
    tokens_major = jnp.moveaxis(scaled.astype(jnp.bfloat16), 0, 1)
    return lax.all_to_all(tokens_major, "head", split_axis=0, concat_axis=1, tiled=True)


def solution(mesh):
    placed = (
        P(("seq", "head"), None, None),
        P(("seq", "head"), None, None, None),
        P(("seq", "head"), None, None, None),
        P("head", None, None),
    )

    def chosen(queries, keys, values, initial_state):
        own_heads = initial_state.shape[0]
        ns, nh = mesh.shape["seq"], mesh.shape["head"]
        fits = own_heads % HEADS_A_STEP == 0 and own_heads * nh % (2 * ns) == 0
        if fits and nh > 1:
            return owned_per_device(queries, keys, values, initial_state)
        return per_device(queries, keys, values, initial_state)

    return jax.shard_map(
        chosen,
        mesh=mesh,
        in_specs=placed,
        out_specs=P(("seq", "head"), None, None),
        check_vma=False,
    )
```

```python
import functools
import itertools

import jax
import jax.numpy as jnp
from jax import lax
from jax.experimental import pallas as pl
from jax.experimental.pallas import tpu as pltpu
from jax.sharding import PartitionSpec as P

BLOCK = 64
BASE = 16
HEADS_A_STEP = 8
UNIT = 4
GROUP = 4
GRAM_SHARE = 0.25
BASE_SHARE = 1.15
VMEM_BYTES = 56 << 20

F32 = jnp.float32
BF16 = jnp.bfloat16
MESH = pl.DeviceIdType.MESH


def mm(left, right, dims=((1,), (0,))):
    return lax.dot_general(left, right, (dims, ((), ())), preferred_element_type=F32)


def split(x):
    high = x.astype(BF16)
    return high, (x - high.astype(F32)).astype(BF16)


def cat(parts, axis):
    return jnp.concatenate(parts, axis=axis)


def exact_left(left, right):
    high, low = split(right)
    return mm(cat([left, left], 1), cat([high, low], 0))


def exact_right(left, right):
    high, low = split(left)
    return mm(cat([high, low], 1), cat([right, right], 0))


def both_split(lh, ll, rh, rl):
    return mm(cat([lh, ll], 1), cat([rh, rh], 0)) + mm(lh, rl)


def both(left, right):
    return both_split(*split(left), *split(right))


def odd_rows(x, size):
    rows = x.shape[0]
    return cat([x[s : s + size] for s in range(size, rows, 2 * size)], 0)


def merge_rows(even_from, odd, size):
    rows = even_from.shape[0]
    parts = []
    for i, s in enumerate(range(0, rows, 2 * size)):
        parts += [even_from[s : s + size], odd[i * size : (i + 1) * size]]
    return cat(parts, 0)


def twice(pair, right_high, right_low):
    k = right_high.shape[0]
    return mm(pair, cat([right_high, right_high], 0)) + mm(pair[:, :k], right_low)


def grams(q_ref, k_ref, v_ref, picked, kq_ref, v_own, x_ref, m_ref, d_ref, seen_ref):
    tokens, _, width = q_ref.shape
    per_token = k_ref.shape[2]
    step = min(BLOCK, tokens)
    n = step * per_token
    row = lax.broadcasted_iota(jnp.int32, (n, n), 0)
    col = lax.broadcasted_iota(jnp.int32, (n, n), 1)
    trow = lax.broadcasted_iota(jnp.int32, (step, n), 0)
    tcol = lax.broadcasted_iota(jnp.int32, (step, n), 1)
    visible = tcol < (trow + 1) * per_token
    for b in range(tokens // step):
        for j, h in enumerate(picked):
            i = b * len(picked) + j
            here = slice(b * step, (b + 1) * step)
            k = k_ref[here, h].reshape(n, width)
            kq = cat([k, q_ref[here, h]], 0)
            kq_ref[i] = kq
            v_own[i] = v_ref[here, h].reshape(n, width)
            gs = mm(kq, k, ((1,), (1,)))
            gram = gs[:n]
            diag = jnp.where(row == col, gram, 0.0)
            norm = jnp.sum(diag, axis=1, keepdims=True) + 1e-06
            d_ref[i] = lax.rsqrt(jnp.sum(diag, axis=0, keepdims=True) + 1e-06)
            d_col = lax.rsqrt(norm)
            x = jnp.where(col < row, (2.0 * d_col * d_col) * gram, 0.0)
            x_ref[i] = cat(split(x), 1)
            seen_ref[i] = cat(split(jnp.where(visible, gs[n:], 0.0)), 1)
            packed = jnp.where(col[:BASE] < BASE, x[:BASE], 0.0)
            for s in range(BASE, n, BASE):
                inside = (col[:BASE] >= s) & (col[:BASE] < s + BASE)
                packed = jnp.where(inside, x[s : s + BASE], packed)
            m_ref[i] = packed
            yield


def base_inverses(m_ref):
    blocks, _, n = m_ref.shape
    sub = lax.broadcasted_iota(jnp.int32, (BASE, n), 0)
    lane = lax.broadcasted_iota(jnp.int32, (BASE, n), 1)
    invs = [jnp.where(sub == lane % BASE, 1.0, 0.0)] * blocks
    for j in range(BASE - 1):
        at = lane - lane % BASE + j
        for i in range(blocks):
            coef = jnp.take_along_axis(m_ref[i], at, axis=1)
            invs[i] = invs[i] - coef * invs[i][j : j + 1]
            if i % GROUP == GROUP - 1:
                yield
    for i, inv in enumerate(invs):
        m_ref[i] = inv


def inverses(v_own, x_ref, m_ref, d_ref, near_ref, fed_ref):
    blocks, n, _ = near_ref.shape
    row = lax.broadcasted_iota(jnp.int32, (n, n), 0)
    col = lax.broadcasted_iota(jnp.int32, (n, n), 1)
    same = row // BASE == col // BASE
    every = range(blocks)
    ms = [jnp.where(same, cat([m_ref[i]] * (n // BASE), 0), 0.0) for i in every]
    size = BASE
    while size < n:
        near = odd_rows(col // size - row // size, size) == -1
        halves, ys = [], []
        for i in every:
            halves.append(split(ms[i]))
            ys.append(twice(odd_rows(x_ref[i], size), *halves[i]))
            if i % GROUP == GROUP - 1:
                yield
        for i in every:
            y = jnp.where(near, ys[i], 0.0)
            ys[i] = split(merge_rows(jnp.zeros((n, n), F32), y, size))
            if i % GROUP == GROUP - 1:
                yield
        for i in every:
            mh, ml = halves[i]
            z = both_split(odd_rows(mh, size), odd_rows(ml, size), *ys[i])
            ms[i] = merge_rows(ms[i], odd_rows(ms[i], size) - z, size)
            if i % GROUP == GROUP - 1:
                yield
        size *= 2
    for i in every:
        d = d_ref[i]
        fed_ref[i] = exact_right(ms[i] * (2.0 * d), v_own[i])
        near_ref[i] = cat(split(ms[i] * (2.0 * d * d)), 1)
        if i % GROUP == GROUP - 1:
            yield


def local_maps(
    heads, kq_ref, near_ref, fed_ref, seen_ref, local_ref, gain_ref, t_ref, a_ref, first
):
    _, rows, width = kq_ref.shape
    n = near_ref.shape[1]
    step = rows - n
    count = kq_ref.shape[0] // heads
    row = lax.broadcasted_iota(jnp.int32, (width, width), 0)
    col = lax.broadcasted_iota(jnp.int32, (width, width), 1)
    eye = jnp.where(row == col, 1.0, 0.0)
    pairs = [cat([jnp.zeros((width, width), F32), eye], 1)] * heads
    for b in range(count):
        at = range(b * heads, (b + 1) * heads)
        if b == 0:
            passed, feeds = [], []
            for i in at:
                kq = kq_ref[i]
                q = kq[n:].astype(F32)
                passed.append(cat([jnp.zeros_like(q), q], 1))
                feeds.append(cat([fed_ref[i], -mm(near_ref[i], cat([kq[:n], kq[:n]], 0))], 1))
                yield
        else:
            aheads = []
            for i, pair in zip(at, pairs):
                aheads.append(exact_left(kq_ref[i], pair))
                yield
            passed = [ahead[n:] for ahead in aheads]
            feeds = []
            for i, ahead in zip(at, aheads):
                fed = cat([fed_ref[i], jnp.zeros((n, width), F32)], 1)
                feeds.append(fed - twice(near_ref[i], *split(ahead[:n])))
                yield
        feeds = [split(feed) for feed in feeds]
        made = []
        for i, pair, feed in zip(at, pairs, feeds):
            k = kq_ref[i, :n]
            made.append(pair + mm(cat([k, k], 0), cat(list(feed), 0), ((0,), (0,))))
            yield
        pairs = made
        for h, (i, base, feed) in enumerate(zip(at, passed, feeds)):
            out = base + twice(seen_ref[i], *feed)
            local_ref[first + h, b * step : (b + 1) * step] = out[:, :width]
            gain_ref[first + h, b * step : (b + 1) * step] = out[:, width:]
            yield
    for h, pair in enumerate(pairs):
        t_ref[first + h] = pair[:, width:]
        a_ref[first + h] = pair[:, :width].astype(a_ref.dtype)


def weave(mains, sides, share):
    owed = 0.0
    for _ in mains:
        owed += share
        while owed >= 1.0:
            owed -= 1.0
            next(sides, None)


def landed(ref, at, sem):
    pltpu.make_async_copy(ref.at[at], ref.at[at], sem.at[at]).wait()


def mixer_kernel(
    ns,
    nh,
    q_ref,
    k_ref,
    v_ref,
    init_ref,
    out_ref,
    local,
    gain,
    t_own,
    a_own,
    t_box,
    a_box,
    t_out,
    a_out,
    t_line,
    a_line,
    s_line,
    s_in,
    s_fwd,
    init_box,
    t_send,
    a_send,
    t_recv,
    a_recv,
    tl_recv,
    al_recv,
    sl_send,
    s_send,
    s_recv,
    i_send,
    i_recv,
    *stages,
):
    size, width = q_ref.shape[1], q_ref.shape[2]
    heads = out_ref.shape[0]
    step = pl.program_id(0)
    s, z = lax.axis_index("seq"), lax.axis_index("head")
    n = ns * nh
    me = s * nh + z
    way = UNIT // 2
    ticks = heads // UNIT
    ends = (0, nh - 1)
    at_end = (z == 0) | (z == nh - 1)

    def place(p):
        return p // nh, lax.rem(p, nh)

    def head_of(group, up, j):
        return group * UNIT + up * way + j

    def slot_of(group, j):
        index = group * way + j
        turn = lax.rem(index, ns)
        half = turn // 2
        return jnp.where(lax.rem(turn, 2) == 0, half, ns - 1 - half), index // ns

    def remote(src, dst, send, recv, where):
        return pltpu.make_async_remote_copy(
            src_ref=src,
            dst_ref=dst,
            send_sem=send,
            recv_sem=recv,
            device_id=where,
            device_id_type=MESH,
        )

    def hop(h, up, t_src, a_src):
        where = (s, z + 1 if up else z - 1)
        return [
            remote(t_src.at[h], t_box.at[h], t_send.at[h], t_recv.at[h], where),
            remote(a_src.at[h], a_box.at[h], a_send.at[h], a_recv.at[h], where),
        ]

    def to_owner(h, owner, slot):
        where = (owner, z)
        return [
            remote(
                t_out.at[h], t_line.at[slot, s], t_send.at[h], tl_recv.at[slot, s], where
            ),
            remote(
                a_out.at[h], a_line.at[slot, s], a_send.at[h], al_recv.at[slot, s], where
            ),
        ]

    def from_owner(h, slot, line):
        return remote(
            s_line.at[slot, line], s_in.at[h], sl_send.at[slot, line], s_recv.at[h], (line, z)
        )

    def state_hop(h, up, src):
        where = (s, z - 1 if up else z + 1)
        return remote(src.at[h], s_in.at[h], s_send.at[h], s_recv.at[h], where)

    def place_of(up):
        return z if up else nh - 1 - z

    def group_at(tick, up):
        spot = place_of(up)
        group = tick - spot
        return group, (spot > 0) & (group >= 0) & (group < ticks)

    def join(todo):
        places = [(head_of(group, up, j), up, group, j) for group, up, j in todo]
        for h, *_ in places:
            landed(t_box, h, t_recv)
            landed(a_box, h, a_recv)
        for h, up, _, _ in places:
            if up:
                later_t, later_a, sooner_t, sooner_a = t_own, a_own, t_box, a_box
            else:
                later_t, later_a, sooner_t, sooner_a = t_box, a_box, t_own, a_own
            high, low = split(later_t[h])
            right_high, right_low = split(sooner_t[h])
            right = cat([right_high, sooner_a[h]], 1)
            made = mm(cat([high, low], 1), cat([right, right], 0))
            t_out[h] = made[:, :width] + mm(high, right_low)
            a_out[h] = (made[:, width:] + later_a[h].astype(F32)).astype(a_out.dtype)
        for h, up, group, j in places:
            spot = place_of(up)
            owner, slot = slot_of(group, j)

            @pl.when(spot < nh - 1)
            def _():
                for copy in hop(h, up, t_out, a_out):
                    copy.start()

            @pl.when((spot == nh - 1) & (owner != s) & (s < ns - 1))
            def _():
                for copy in to_owner(h, owner, slot):
                    copy.start()

            @pl.when((spot == nh - 1) & (owner == s) & (s < ns - 1))
            def _():
                pltpu.make_async_copy(
                    t_out.at[h], t_line.at[slot, s], tl_recv.at[slot, s]
                ).start()
                pltpu.make_async_copy(
                    a_out.at[h], a_line.at[slot, s], al_recv.at[slot, s]
                ).start()

    def compose(tick):
        (down, down_on), (raised, up_on) = group_at(tick, 0), group_at(tick, 1)

        @pl.when(down_on & up_on)
        def _():
            join([(raised, 1, j) for j in range(way)] + [(down, 0, j) for j in range(way)])

        @pl.when(down_on & ~up_on)
        def _():
            join([(down, 0, j) for j in range(way)])

        @pl.when(up_on & ~down_on)
        def _():
            join([(raised, 1, j) for j in range(way)])

    def compose_singly(tick):
        for j in range(way):
            for up in (1, 0):
                group, on = group_at(tick, up)

                @pl.when(on)
                def _():
                    join([(group, up, j)])

    def chain(tick):
        group = tick - nh
        turn = jnp.where(s < ns // 2, 2 * s, 2 * (ns - 1 - s) + 1)
        j = lax.rem(turn + ns * ticks * way - group * way, ns)

        @pl.when(at_end & (group >= 0) & (group < ticks) & (j < way))
        def _():
            slot = (group * way + j) // ns
            h = group * UNIT + jnp.where(z == 0, 0, way) + j
            landed(init_box, slot, i_recv)

            def send(line, state):
                s_line[slot, line] = state.astype(s_line.dtype)

                @pl.when(line != s)
                def _():
                    from_owner(h, slot, line).start()

                @pl.when(line == s)
                def _():
                    pltpu.make_async_copy(
                        s_line.at[slot, line], s_in.at[h], s_recv.at[h]
                    ).start()

            def advance(line, state):
                send(line, state)
                landed(t_line, (slot, line), tl_recv)
                landed(a_line, (slot, line), al_recv)
                return both(t_line[slot, line], state) + a_line[slot, line].astype(F32)

            send(ns - 1, lax.fori_loop(0, ns - 1, advance, init_box[slot], unroll=True))

    def finish(h, read):
        raw = local[h] + read
        mean = jnp.mean(raw * raw, axis=-1, keepdims=True)
        out_ref[h] = (raw * lax.rsqrt(mean + 1e-06)).astype(out_ref.dtype)

    def settle(tick, up):
        spot = place_of(up)
        group = tick - 2 * nh + spot

        @pl.when((group >= 0) & (group < ticks))
        def _():
            picked = [head_of(group, up, j) for j in range(way)]
            if up:

                @pl.when(spot > 0)
                def _():
                    for h in picked:
                        landed(s_in, h, s_recv)
                        state_hop(h, up, s_in).start()
                    for h in picked:
                        state = exact_right(t_box[h], s_in[h]) + a_box[h].astype(F32)
                        finish(h, both(gain[h], state))

                @pl.when(spot == 0)
                def _():
                    for h in picked:
                        landed(s_in, h, s_recv)
                    for h in picked:
                        finish(h, exact_right(gain[h], s_in[h]))

            else:
                for h in picked:
                    landed(s_in, h, s_recv)

                @pl.when(spot > 0)
                def _():
                    for h in picked:
                        state = exact_right(t_own[h], s_in[h]) + a_own[h].astype(F32)
                        s_fwd[h] = state.astype(BF16)
                        state_hop(h, up, s_fwd).start()

                for h in picked:
                    finish(h, exact_right(gain[h], s_in[h]))

    def exchange(tick, pieces=compose):
        pieces(tick)
        chain(tick)
        for up in (0, 1):
            settle(tick, up)

    own = init_ref.shape[0]

    def init_copies():
        for i in range(own):
            h = z * own + i
            up = (i % UNIT) // way
            owner, slot = slot_of(h // UNIT, i % way)
            copy = remote(
                init_ref.at[i], init_box.at[slot], i_send.at[i], i_recv.at[slot], (s, ends[up])
            )
            yield i, up, owner, slot, copy

    @pl.when(step == 0)
    def _():
        barrier = pltpu.get_barrier_semaphore()

        @pl.loop(1, n)
        def _(i):
            pl.semaphore_signal(
                barrier, inc=1, device_id=place(lax.rem(me + i, n)), device_id_type=MESH
            )

    subs = size // UNIT
    kept = len(stages) // subs

    def stage_of(sub):
        return stages[sub * kept : (sub + 1) * kept]

    def picked_of(sub):
        return list(range(sub * UNIT, (sub + 1) * UNIT))

    def advance_maps(done, first, later):
        none = iter(())
        invert, carry, gram, base = none, none, none, none
        if done is not None:
            kq, near, fed, seen, v_own, x, m, d = stage_of(done)
            invert = inverses(v_own, x, m, d, near, fed)
            carry = local_maps(
                UNIT, kq, near, fed, seen, local, gain, t_own, a_own, first
            )
        if later is not None:
            kq, near, fed, seen, v_own, x, m, d = stage_of(later)
            gram = grams(
                q_ref, k_ref, v_ref, picked_of(later), kq, v_own, x, m, d, seen
            )
            base = base_inverses(m)
        sides = itertools.chain(gram, base)
        weave(invert, sides, GRAM_SHARE)
        weave(carry, sides, BASE_SHARE)
        for _ in sides:
            pass

    def offer(first):
        for up in (0, 1):

            @pl.when(place_of(up) == 0)
            def _():
                for j in range(way):
                    for copy in hop(first + up * way + j, up, t_own, a_own):
                        copy.start()

    @pl.when(step == 0)
    def _():
        advance_maps(None, None, 0)
        pl.semaphore_wait(pltpu.get_barrier_semaphore(), n - 1)
        for i, up, owner, slot, copy in init_copies():

            @pl.when((owner == s) & (z != ends[up]))
            def _():
                copy.start()

            @pl.when((owner == s) & (z == ends[up]))
            def _():
                pltpu.make_async_copy(
                    init_ref.at[i], init_box.at[slot], i_recv.at[slot]
                ).start()

    @pl.when(step > 0)
    def _():
        advance_maps(subs - 1, step * size - UNIT, 0)
        offer(step * size - UNIT)
        exchange(step * subs - 1)

    for sub in range(1, subs):
        advance_maps(sub - 1, step * size + (sub - 1) * UNIT, sub)
        offer(step * size + (sub - 1) * UNIT)
        exchange(step * subs + sub - 1)

    @pl.when(step == pl.num_programs(0) - 1)
    def _():
        advance_maps(subs - 1, heads - UNIT, None)
        offer(heads - UNIT)

        @pl.loop(ticks - 1, ticks + 2 * nh)
        def _(tick):
            exchange(tick, compose_singly)

        for i, up, owner, slot, copy in init_copies():

            @pl.when((owner == s) & (z != ends[up]))
            def _():
                copy.wait_send()

        @pl.loop(0, ticks)
        def _(group):
            for up in (0, 1):
                spot = place_of(up)
                for j in range(way):
                    h = head_of(group, up, j)
                    owner, slot = slot_of(group, j)

                    @pl.when(spot < nh - 1)
                    def _():
                        for copy in hop(h, up, t_out, a_out):
                            copy.wait_send()

                    @pl.when((spot == nh - 1) & (owner != s) & (s < ns - 1))
                    def _():
                        for copy in to_owner(h, owner, slot):
                            copy.wait_send()

                    @pl.when(spot > 0)
                    def _():
                        state_hop(h, up, s_fwd).wait_send()

                    @pl.when((spot == nh - 1) & (owner == s))
                    def _():
                        @pl.loop(0, ns)
                        def _(line):
                            @pl.when(line != s)
                            def _():
                                from_owner(h, slot, line).wait_send()


def mixer(q, k, v, initial_state):
    ns, nh = lax.axis_size("seq"), lax.axis_size("head")
    tokens, heads, width = q.shape
    g = HEADS_A_STEP
    slots = heads // (2 * ns)
    dma = pltpu.SemaphoreType.DMA

    def by_token(rows):
        return pl.BlockSpec((tokens, g, rows, width), lambda i: (0, i, 0, 0))

    def maps(*lead):
        square = (*lead, width, width)
        return [pltpu.VMEM(square, F32), pltpu.VMEM(square, BF16)]

    step = min(BLOCK, tokens)
    n = step * k.shape[2]
    blocks = UNIT * (tokens // step)
    stage = [
        pltpu.VMEM((blocks, n + step, width), BF16),
        pltpu.VMEM((blocks, n, 2 * n), BF16),
        pltpu.VMEM((blocks, n, width), F32),
        pltpu.VMEM((blocks, step, 2 * n), BF16),
        pltpu.VMEM((blocks, n, width), BF16),
        pltpu.VMEM((blocks, n, 2 * n), BF16),
        pltpu.VMEM((blocks, BASE, n), F32),
        pltpu.VMEM((blocks, 1, n), F32),
    ]
    return pl.pallas_call(
        functools.partial(mixer_kernel, ns, nh),
        grid=(heads // g,),
        in_specs=[
            pl.BlockSpec((tokens, g, width), lambda i: (0, i, 0)),
            by_token(k.shape[2]),
            by_token(k.shape[2]),
            pl.BlockSpec(initial_state.shape, lambda i: (0, 0, 0)),
        ],
        out_specs=pl.BlockSpec((heads, tokens, width), lambda i: (0, 0, 0)),
        out_shape=jax.ShapeDtypeStruct((heads, tokens, width), BF16),
        scratch_shapes=[
            pltpu.VMEM((heads, tokens, width), F32),
            pltpu.VMEM((heads, tokens, width), F32),
            *maps(heads),
            *maps(heads),
            *maps(heads),
            *maps(slots, ns),
            pltpu.VMEM((slots, ns, width, width), BF16),
            pltpu.VMEM((heads, width, width), BF16),
            pltpu.VMEM((heads, width, width), BF16),
            pltpu.VMEM((slots, width, width), F32),
            dma((heads,)),
            dma((heads,)),
            dma((heads,)),
            dma((heads,)),
            dma((slots, ns)),
            dma((slots, ns)),
            dma((slots, ns)),
            dma((heads,)),
            dma((heads,)),
            dma((initial_state.shape[0],)),
            dma((slots,)),
            *stage * (g // UNIT),
        ],
        compiler_params=pltpu.CompilerParams(
            collective_id=0, has_side_effects=True, vmem_limit_bytes=VMEM_BYTES
        ),
        name="mixer",
    )(q, k, v, initial_state)


def owned_per_device(queries, keys, values, initial_state):
    tokens, heads, width = queries.shape
    return jnp.swapaxes(mixer(queries, keys, values, initial_state), 0, 1)


HIGH = lax.Precision.HIGHEST


def shifted(value, axis, by):
    size = lax.axis_size(axis)
    pairs = [(i, i + by) for i in range(size) if 0 <= i + by < size]
    return lax.ppermute(value, axis, pairs)


def matmul(left, right):
    return jnp.dot(left, right, precision=HIGH, preferred_element_type=jnp.float32)


def batched(left, right):
    return jnp.einsum("hij,hjk->hik", left, right, precision=HIGH)


def unit_rows(raw_keys):
    floats = raw_keys.astype(jnp.float32)
    return floats * lax.rsqrt(jnp.sum(floats * floats, axis=-1, keepdims=True) + 1e-06)


def all_factors(k_blocks, v_blocks):
    updates = k_blocks.shape[2]
    head_width = k_blocks.shape[3]
    gram = jnp.einsum("hbid,hbjd->hbij", k_blocks, k_blocks, precision=HIGH)
    system = jnp.eye(updates, dtype=jnp.float32) + jnp.tril(2.0 * gram, -1)
    solved = lax.linalg.triangular_solve(
        system,
        2.0 * jnp.concatenate([k_blocks, v_blocks], axis=-1),
        left_side=True,
        lower=True,
        unit_diagonal=True,
    )
    return (solved[..., :head_width], solved[..., head_width:])


def visible_scores(q_blk, k_blk):
    rows = q_blk.shape[0]
    updates = k_blk.shape[0]
    per_token = updates // rows
    row_ids = lax.broadcasted_iota(jnp.int32, (rows, updates), 0)
    col_ids = lax.broadcasted_iota(jnp.int32, (rows, updates), 1)
    return jnp.where(col_ids < (row_ids + 1) * per_token, matmul(q_blk, k_blk.T), 0.0)


def start_pair(head_width):
    return jnp.concatenate(
        [jnp.zeros((head_width, head_width), jnp.float32), jnp.eye(head_width, dtype=jnp.float32)],
        axis=1,
    )


def carried_pass(q_blocks, k_blocks, w_blocks, u_blocks):
    head_width = q_blocks.shape[2]

    def advance(pair_state, block_item):
        q_blk, k_blk, w_mat, u_mat = block_item
        feed_rows = jnp.concatenate([u_mat, jnp.zeros_like(u_mat)], axis=1) - matmul(
            w_mat, pair_state
        )
        outputs = matmul(q_blk, pair_state) + matmul(visible_scores(q_blk, k_blk), feed_rows)
        return (pair_state + matmul(k_blk.T, feed_rows), outputs)

    final_pair, outputs = lax.scan(
        advance, start_pair(head_width), (q_blocks, k_blocks, w_blocks, u_blocks)
    )
    outputs = outputs.reshape(-1, 2 * head_width)
    return (
        final_pair[:, head_width:],
        final_pair[:, :head_width],
        outputs[:, :head_width],
        outputs[:, head_width:],
    )


def per_device(queries, keys, values, initial_state):
    q_heads, k_heads, v_heads = (
        lax.all_to_all(queries, "head", split_axis=1, concat_axis=0, tiled=True),
        lax.all_to_all(keys, "head", split_axis=1, concat_axis=0, tiled=True),
        lax.all_to_all(values, "head", split_axis=1, concat_axis=0, tiled=True),
    )
    head_width = q_heads.shape[2]
    local_heads = q_heads.shape[1]
    blocks = q_heads.shape[0] // BLOCK
    q_blocks = jnp.moveaxis(q_heads.astype(jnp.float32), 1, 0).reshape(
        local_heads, blocks, BLOCK, head_width
    )
    k_blocks = jnp.moveaxis(unit_rows(k_heads), 1, 0).reshape(local_heads, blocks, -1, head_width)
    v_blocks = jnp.moveaxis(v_heads.astype(jnp.float32), 1, 0).reshape(
        local_heads, blocks, -1, head_width
    )
    w_blocks, u_blocks = all_factors(k_blocks, v_blocks)
    transition, additive, local_out, query_gain = jax.vmap(carried_pass)(
        q_blocks, k_blocks, w_blocks, u_blocks
    )
    at_first = lax.axis_index("seq") == 0
    start_state = jnp.where(at_first, initial_state, jnp.zeros_like(initial_state))

    def relay_step(loop_step, current):
        passed = shifted(batched(transition, current) + additive, "seq", 1)
        return jnp.where(at_first, initial_state, passed)

    incoming = lax.fori_loop(0, lax.axis_size("seq") - 1, relay_step, start_state)
    raw_out = local_out + batched(query_gain, incoming)
    scaled = raw_out * lax.rsqrt(jnp.mean(raw_out * raw_out, axis=-1, keepdims=True) + 1e-06)
    tokens_major = jnp.moveaxis(scaled.astype(jnp.bfloat16), 0, 1)
    return lax.all_to_all(tokens_major, "head", split_axis=0, concat_axis=1, tiled=True)


def solution(mesh):
    placed = (
        P(("seq", "head"), None, None),
        P(("seq", "head"), None, None, None),
        P(("seq", "head"), None, None, None),
        P("head", None, None),
    )

    def chosen(queries, keys, values, initial_state):
        own_heads = initial_state.shape[0]
        ns, nh = mesh.shape["seq"], mesh.shape["head"]
        fits = own_heads % HEADS_A_STEP == 0 and own_heads * nh % (2 * ns) == 0
        if fits and nh > 1:
            return owned_per_device(queries, keys, values, initial_state)
        return per_device(queries, keys, values, initial_state)

    return jax.shard_map(
        chosen,
        mesh=mesh,
        in_specs=placed,
        out_specs=P(("seq", "head"), None, None),
        check_vma=False,
    )
```

```python
import functools
import itertools

import jax
import jax.numpy as jnp
from jax import lax
from jax.experimental import pallas as pl
from jax.experimental.pallas import tpu as pltpu
from jax.sharding import PartitionSpec as P

BLOCK = 64
BASE = 16
HEADS_A_STEP = 8
UNIT = 4
GROUP = 4
GRAM_SHARE = 0.25
BASE_SHARE = 1.15
VMEM_BYTES = 56 << 20

F32 = jnp.float32
BF16 = jnp.bfloat16
MESH = pl.DeviceIdType.MESH


def mm(left, right, dims=((1,), (0,))):
    return lax.dot_general(left, right, (dims, ((), ())), preferred_element_type=F32)


def split(x):
    high = x.astype(BF16)
    return high, (x - high.astype(F32)).astype(BF16)


def cat(parts, axis):
    return jnp.concatenate(parts, axis=axis)


def exact_left(left, right):
    high, low = split(right)
    return mm(cat([left, left], 1), cat([high, low], 0))


def exact_right(left, right):
    high, low = split(left)
    return mm(cat([high, low], 1), cat([right, right], 0))


def both_split(lh, ll, rh, rl):
    return mm(cat([lh, ll], 1), cat([rh, rh], 0)) + mm(lh, rl)


def both(left, right):
    return both_split(*split(left), *split(right))


def odd_rows(x, size):
    rows = x.shape[0]
    return cat([x[s : s + size] for s in range(size, rows, 2 * size)], 0)


def merge_rows(even_from, odd, size):
    rows = even_from.shape[0]
    parts = []
    for i, s in enumerate(range(0, rows, 2 * size)):
        parts += [even_from[s : s + size], odd[i * size : (i + 1) * size]]
    return cat(parts, 0)


def twice(pair, right_high, right_low):
    k = right_high.shape[0]
    return mm(pair, cat([right_high, right_high], 0)) + mm(pair[:, :k], right_low)


def grams(q_ref, k_ref, v_ref, q_rows, picked, kq_ref, v_own, x_ref, m_ref, d_ref, seen_ref):
    tokens, size, width = q_ref.shape
    per_token = k_ref.shape[2]
    step = min(BLOCK, tokens)
    n = step * per_token
    row = lax.broadcasted_iota(jnp.int32, (n, n), 0)
    col = lax.broadcasted_iota(jnp.int32, (n, n), 1)
    trow = lax.broadcasted_iota(jnp.int32, (step, n), 0)
    tcol = lax.broadcasted_iota(jnp.int32, (step, n), 1)
    visible = tcol < (trow + 1) * per_token
    for b in range(tokens // step):
        if picked[0] == 0:
            q = q_ref[b * step : (b + 1) * step].astype(F32)
            q_rows[b * step * size : (b + 1) * step * size] = q.reshape(-1, width)
        for j, h in enumerate(picked):
            i = b * len(picked) + j
            here = slice(b * step, (b + 1) * step)
            k = k_ref[here, h].reshape(n, width)
            q = q_rows[pl.ds(b * step * size + h, step, stride=size)]
            kq = cat([k, q.astype(BF16)], 0)
            kq_ref[i] = kq
            v_own[i] = v_ref[here, h].reshape(n, width)
            gs = mm(kq, k, ((1,), (1,)))
            gram = gs[:n]
            diag = jnp.where(row == col, gram, 0.0)
            norm = jnp.sum(diag, axis=1, keepdims=True) + 1e-06
            d_ref[i] = lax.rsqrt(jnp.sum(diag, axis=0, keepdims=True) + 1e-06)
            d_col = lax.rsqrt(norm)
            x = jnp.where(col < row, (2.0 * d_col * d_col) * gram, 0.0)
            x_ref[i] = cat(split(x), 1)
            seen_ref[i] = cat(split(jnp.where(visible, gs[n:], 0.0)), 1)
            packed = jnp.where(col[:BASE] < BASE, x[:BASE], 0.0)
            for s in range(BASE, n, BASE):
                inside = (col[:BASE] >= s) & (col[:BASE] < s + BASE)
                packed = jnp.where(inside, x[s : s + BASE], packed)
            m_ref[i] = packed
            yield


def base_inverses(m_ref):
    blocks, _, n = m_ref.shape
    sub = lax.broadcasted_iota(jnp.int32, (BASE, n), 0)
    lane = lax.broadcasted_iota(jnp.int32, (BASE, n), 1)
    invs = [jnp.where(sub == lane % BASE, 1.0, 0.0)] * blocks
    for j in range(BASE - 1):
        at = lane - lane % BASE + j
        for i in range(blocks):
            coef = jnp.take_along_axis(m_ref[i], at, axis=1)
            invs[i] = invs[i] - coef * invs[i][j : j + 1]
            if i % GROUP == GROUP - 1:
                yield
    for i, inv in enumerate(invs):
        m_ref[i] = inv


def inverses(v_own, x_ref, m_ref, d_ref, near_ref, fed_ref):
    blocks, n, _ = near_ref.shape
    row = lax.broadcasted_iota(jnp.int32, (n, n), 0)
    col = lax.broadcasted_iota(jnp.int32, (n, n), 1)
    same = row // BASE == col // BASE
    every = range(blocks)
    ms = [jnp.where(same, cat([m_ref[i]] * (n // BASE), 0), 0.0) for i in every]
    size = BASE
    while size < n:
        near = odd_rows(col // size - row // size, size) == -1
        halves, ys = [], []
        for i in every:
            halves.append(split(ms[i]))
            ys.append(twice(odd_rows(x_ref[i], size), *halves[i]))
            if i % GROUP == GROUP - 1:
                yield
        for i in every:
            y = jnp.where(near, ys[i], 0.0)
            ys[i] = split(merge_rows(jnp.zeros((n, n), F32), y, size))
            if i % GROUP == GROUP - 1:
                yield
        for i in every:
            mh, ml = halves[i]
            z = both_split(odd_rows(mh, size), odd_rows(ml, size), *ys[i])
            ms[i] = merge_rows(ms[i], odd_rows(ms[i], size) - z, size)
            if i % GROUP == GROUP - 1:
                yield
        size *= 2
    for i in every:
        d = d_ref[i]
        fed_ref[i] = exact_right(ms[i] * (2.0 * d), v_own[i])
        near_ref[i] = cat(split(ms[i] * (2.0 * d * d)), 1)
        if i % GROUP == GROUP - 1:
            yield


def local_maps(
    heads, kq_ref, near_ref, fed_ref, seen_ref, local_ref, gain_ref, t_ref, a_ref, first
):
    _, rows, width = kq_ref.shape
    n = near_ref.shape[1]
    step = rows - n
    count = kq_ref.shape[0] // heads
    row = lax.broadcasted_iota(jnp.int32, (width, width), 0)
    col = lax.broadcasted_iota(jnp.int32, (width, width), 1)
    eye = jnp.where(row == col, 1.0, 0.0)
    pairs = [cat([jnp.zeros((width, width), F32), eye], 1)] * heads
    for b in range(count):
        at = range(b * heads, (b + 1) * heads)
        if b == 0:
            passed, feeds = [], []
            for i in at:
                kq = kq_ref[i]
                q = kq[n:].astype(F32)
                passed.append(cat([jnp.zeros_like(q), q], 1))
                feeds.append(cat([fed_ref[i], -mm(near_ref[i], cat([kq[:n], kq[:n]], 0))], 1))
                yield
        else:
            aheads = []
            for i, pair in zip(at, pairs):
                aheads.append(exact_left(kq_ref[i], pair))
                yield
            passed = [ahead[n:] for ahead in aheads]
            feeds = []
            for i, ahead in zip(at, aheads):
                fed = cat([fed_ref[i], jnp.zeros((n, width), F32)], 1)
                feeds.append(fed - twice(near_ref[i], *split(ahead[:n])))
                yield
        feeds = [split(feed) for feed in feeds]
        made = []
        for i, pair, feed in zip(at, pairs, feeds):
            k = kq_ref[i, :n]
            made.append(pair + mm(cat([k, k], 0), cat(list(feed), 0), ((0,), (0,))))
            yield
        pairs = made
        for h, (i, base, feed) in enumerate(zip(at, passed, feeds)):
            out = base + twice(seen_ref[i], *feed)
            local_ref[first + h, b * step : (b + 1) * step] = out[:, :width]
            gain_ref[first + h, b * step : (b + 1) * step] = out[:, width:]
            yield
    for h, pair in enumerate(pairs):
        t_ref[first + h] = pair[:, width:]
        a_ref[first + h] = pair[:, :width].astype(a_ref.dtype)


def weave(mains, sides, share):
    owed = 0.0
    for _ in mains:
        owed += share
        while owed >= 1.0:
            owed -= 1.0
            next(sides, None)


def landed(ref, at, sem):
    pltpu.make_async_copy(ref.at[at], ref.at[at], sem.at[at]).wait()


def mixer_kernel(
    ns,
    nh,
    q_ref,
    k_ref,
    v_ref,
    init_ref,
    out_ref,
    local,
    gain,
    t_own,
    a_own,
    t_box,
    a_box,
    t_out,
    a_out,
    t_line,
    a_line,
    s_line,
    s_in,
    s_fwd,
    init_box,
    t_send,
    a_send,
    t_recv,
    a_recv,
    tl_recv,
    al_recv,
    sl_send,
    s_send,
    s_recv,
    i_send,
    i_recv,
    q_rows,
    *stages,
):
    size, width = q_ref.shape[1], q_ref.shape[2]
    heads = out_ref.shape[0]
    step = pl.program_id(0)
    s, z = lax.axis_index("seq"), lax.axis_index("head")
    n = ns * nh
    me = s * nh + z
    way = UNIT // 2
    ticks = heads // UNIT
    ends = (0, nh - 1)
    at_end = (z == 0) | (z == nh - 1)

    def place(p):
        return p // nh, lax.rem(p, nh)

    def head_of(group, up, j):
        return group * UNIT + up * way + j

    def slot_of(group, j):
        index = group * way + j
        turn = lax.rem(index, ns)
        half = turn // 2
        return jnp.where(lax.rem(turn, 2) == 0, half, ns - 1 - half), index // ns

    def remote(src, dst, send, recv, where):
        return pltpu.make_async_remote_copy(
            src_ref=src,
            dst_ref=dst,
            send_sem=send,
            recv_sem=recv,
            device_id=where,
            device_id_type=MESH,
        )

    def hop(h, up, t_src, a_src):
        where = (s, z + 1 if up else z - 1)
        return [
            remote(t_src.at[h], t_box.at[h], t_send.at[h], t_recv.at[h], where),
            remote(a_src.at[h], a_box.at[h], a_send.at[h], a_recv.at[h], where),
        ]

    def to_owner(h, owner, slot):
        where = (owner, z)
        return [
            remote(
                t_out.at[h], t_line.at[slot, s], t_send.at[h], tl_recv.at[slot, s], where
            ),
            remote(
                a_out.at[h], a_line.at[slot, s], a_send.at[h], al_recv.at[slot, s], where
            ),
        ]

    def from_owner(h, slot, line):
        return remote(
            s_line.at[slot, line], s_in.at[h], sl_send.at[slot, line], s_recv.at[h], (line, z)
        )

    def state_hop(h, up, src):
        where = (s, z - 1 if up else z + 1)
        return remote(src.at[h], s_in.at[h], s_send.at[h], s_recv.at[h], where)

    def place_of(up):
        return z if up else nh - 1 - z

    def group_at(tick, up):
        spot = place_of(up)
        group = tick - spot
        return group, (spot > 0) & (group >= 0) & (group < ticks)

    def join(todo):
        places = [(head_of(group, up, j), up, group, j) for group, up, j in todo]
        for h, *_ in places:
            landed(t_box, h, t_recv)
            landed(a_box, h, a_recv)
        for h, up, _, _ in places:
            if up:
                later_t, later_a, sooner_t, sooner_a = t_own, a_own, t_box, a_box
            else:
                later_t, later_a, sooner_t, sooner_a = t_box, a_box, t_own, a_own
            high, low = split(later_t[h])
            right_high, right_low = split(sooner_t[h])
            right = cat([right_high, sooner_a[h]], 1)
            made = mm(cat([high, low], 1), cat([right, right], 0))
            t_out[h] = made[:, :width] + mm(high, right_low)
            a_out[h] = (made[:, width:] + later_a[h].astype(F32)).astype(a_out.dtype)
        for h, up, group, j in places:
            spot = place_of(up)
            owner, slot = slot_of(group, j)

            @pl.when(spot < nh - 1)
            def _():
                for copy in hop(h, up, t_out, a_out):
                    copy.start()

            @pl.when((spot == nh - 1) & (owner != s) & (s < ns - 1))
            def _():
                for copy in to_owner(h, owner, slot):
                    copy.start()

            @pl.when((spot == nh - 1) & (owner == s) & (s < ns - 1))
            def _():
                pltpu.make_async_copy(
                    t_out.at[h], t_line.at[slot, s], tl_recv.at[slot, s]
                ).start()
                pltpu.make_async_copy(
                    a_out.at[h], a_line.at[slot, s], al_recv.at[slot, s]
                ).start()

    def compose(tick):
        (down, down_on), (raised, up_on) = group_at(tick, 0), group_at(tick, 1)

        @pl.when(down_on & up_on)
        def _():
            join([(raised, 1, j) for j in range(way)] + [(down, 0, j) for j in range(way)])

        @pl.when(down_on & ~up_on)
        def _():
            join([(down, 0, j) for j in range(way)])

        @pl.when(up_on & ~down_on)
        def _():
            join([(raised, 1, j) for j in range(way)])

    def compose_singly(tick):
        for j in range(way):
            for up in (1, 0):
                group, on = group_at(tick, up)

                @pl.when(on)
                def _():
                    join([(group, up, j)])

    def chain(tick):
        group = tick - nh
        turn = jnp.where(s < ns // 2, 2 * s, 2 * (ns - 1 - s) + 1)
        j = lax.rem(turn + ns * ticks * way - group * way, ns)

        @pl.when(at_end & (group >= 0) & (group < ticks) & (j < way))
        def _():
            slot = (group * way + j) // ns
            h = group * UNIT + jnp.where(z == 0, 0, way) + j
            landed(init_box, slot, i_recv)

            def send(line, state):
                s_line[slot, line] = state.astype(s_line.dtype)

                @pl.when(line != s)
                def _():
                    from_owner(h, slot, line).start()

                @pl.when(line == s)
                def _():
                    pltpu.make_async_copy(
                        s_line.at[slot, line], s_in.at[h], s_recv.at[h]
                    ).start()

            def advance(line, state):
                send(line, state)
                landed(t_line, (slot, line), tl_recv)
                landed(a_line, (slot, line), al_recv)
                return both(t_line[slot, line], state) + a_line[slot, line].astype(F32)

            send(ns - 1, lax.fori_loop(0, ns - 1, advance, init_box[slot], unroll=True))

    def finish(h, read):
        raw = local[h] + read
        mean = jnp.mean(raw * raw, axis=-1, keepdims=True)
        out_ref[h] = (raw * lax.rsqrt(mean + 1e-06)).astype(out_ref.dtype)

    def settled_at(tick, up):
        group = tick - 2 * nh + place_of(up)
        return [head_of(group, up, j) for j in range(way)], (group >= 0) & (group < ticks)

    def relay(tick, up):
        picked, on = settled_at(tick, up)

        @pl.when(on)
        def _():
            for h in picked:
                landed(s_in, h, s_recv)

            @pl.when(place_of(up) > 0)
            def _():
                for h in picked:
                    if up:
                        state_hop(h, up, s_in).start()
                    else:
                        state = exact_right(t_own[h], s_in[h]) + a_own[h].astype(F32)
                        s_fwd[h] = state.astype(BF16)
                        state_hop(h, up, s_fwd).start()

    def settle(tick, up):
        picked, on = settled_at(tick, up)
        moved = (place_of(up) > 0) if up else False

        if up:

            @pl.when(on & moved)
            def _():
                for h in picked:
                    state = exact_right(t_box[h], s_in[h]) + a_box[h].astype(F32)
                    finish(h, both(gain[h], state))

        @pl.when(on & ~moved if up else on)
        def _():
            for h in picked:
                finish(h, exact_right(gain[h], s_in[h]))

    def exchange(tick, pieces=compose):
        pieces(tick)
        chain(tick)
        for up in (1, 0):
            relay(tick, up)
        for up in (1, 0):
            settle(tick, up)

    own = init_ref.shape[0]

    def init_copies():
        for i in range(own):
            h = z * own + i
            up = (i % UNIT) // way
            owner, slot = slot_of(h // UNIT, i % way)
            copy = remote(
                init_ref.at[i], init_box.at[slot], i_send.at[i], i_recv.at[slot], (s, ends[up])
            )
            yield i, up, owner, slot, copy

    @pl.when(step == 0)
    def _():
        barrier = pltpu.get_barrier_semaphore()

        @pl.loop(1, n)
        def _(i):
            pl.semaphore_signal(
                barrier, inc=1, device_id=place(lax.rem(me + i, n)), device_id_type=MESH
            )

    subs = size // UNIT
    kept = len(stages) // subs

    def stage_of(sub):
        return stages[sub * kept : (sub + 1) * kept]

    def picked_of(sub):
        return list(range(sub * UNIT, (sub + 1) * UNIT))

    def advance_maps(done, first, later):
        none = iter(())
        invert, carry, gram, base = none, none, none, none
        if done is not None:
            kq, near, fed, seen, v_own, x, m, d = stage_of(done)
            invert = inverses(v_own, x, m, d, near, fed)
            carry = local_maps(
                UNIT, kq, near, fed, seen, local, gain, t_own, a_own, first
            )
        if later is not None:
            kq, near, fed, seen, v_own, x, m, d = stage_of(later)
            gram = grams(
                q_ref, k_ref, v_ref, q_rows, picked_of(later), kq, v_own, x, m, d, seen
            )
            base = base_inverses(m)
        sides = itertools.chain(gram, base)
        weave(invert, sides, GRAM_SHARE)
        weave(carry, sides, BASE_SHARE)
        for _ in sides:
            pass

    def offer(first):
        for up in (0, 1):

            @pl.when(place_of(up) == 0)
            def _():
                for j in range(way):
                    for copy in hop(first + up * way + j, up, t_own, a_own):
                        copy.start()

    @pl.when(step == 0)
    def _():
        advance_maps(None, None, 0)
        pl.semaphore_wait(pltpu.get_barrier_semaphore(), n - 1)
        for i, up, owner, slot, copy in init_copies():

            @pl.when((owner == s) & (z != ends[up]))
            def _():
                copy.start()

            @pl.when((owner == s) & (z == ends[up]))
            def _():
                pltpu.make_async_copy(
                    init_ref.at[i], init_box.at[slot], i_recv.at[slot]
                ).start()

    @pl.when(step > 0)
    def _():
        advance_maps(subs - 1, step * size - UNIT, 0)
        offer(step * size - UNIT)
        exchange(step * subs - 1)

    for sub in range(1, subs):
        advance_maps(sub - 1, step * size + (sub - 1) * UNIT, sub)
        offer(step * size + (sub - 1) * UNIT)
        exchange(step * subs + sub - 1)

    @pl.when(step == pl.num_programs(0) - 1)
    def _():
        advance_maps(subs - 1, heads - UNIT, None)
        offer(heads - UNIT)

        @pl.loop(ticks - 1, ticks + 2 * nh)
        def _(tick):
            exchange(tick, compose_singly)

        for i, up, owner, slot, copy in init_copies():

            @pl.when((owner == s) & (z != ends[up]))
            def _():
                copy.wait_send()

        @pl.loop(0, ticks)
        def _(group):
            for up in (0, 1):
                spot = place_of(up)
                for j in range(way):
                    h = head_of(group, up, j)
                    owner, slot = slot_of(group, j)

                    @pl.when(spot < nh - 1)
                    def _():
                        for copy in hop(h, up, t_out, a_out):
                            copy.wait_send()

                    @pl.when((spot == nh - 1) & (owner != s) & (s < ns - 1))
                    def _():
                        for copy in to_owner(h, owner, slot):
                            copy.wait_send()

                    @pl.when(spot > 0)
                    def _():
                        state_hop(h, up, s_fwd).wait_send()

                    @pl.when((spot == nh - 1) & (owner == s))
                    def _():
                        @pl.loop(0, ns)
                        def _(line):
                            @pl.when(line != s)
                            def _():
                                from_owner(h, slot, line).wait_send()


def mixer(q, k, v, initial_state):
    ns, nh = lax.axis_size("seq"), lax.axis_size("head")
    tokens, heads, width = q.shape
    g = HEADS_A_STEP
    slots = heads // (2 * ns)
    dma = pltpu.SemaphoreType.DMA

    def by_token(rows):
        return pl.BlockSpec((tokens, g, rows, width), lambda i: (0, i, 0, 0))

    def maps(*lead):
        square = (*lead, width, width)
        return [pltpu.VMEM(square, F32), pltpu.VMEM(square, BF16)]

    step = min(BLOCK, tokens)
    n = step * k.shape[2]
    blocks = UNIT * (tokens // step)
    stage = [
        pltpu.VMEM((blocks, n + step, width), BF16),
        pltpu.VMEM((blocks, n, 2 * n), BF16),
        pltpu.VMEM((blocks, n, width), F32),
        pltpu.VMEM((blocks, step, 2 * n), BF16),
        pltpu.VMEM((blocks, n, width), BF16),
        pltpu.VMEM((blocks, n, 2 * n), BF16),
        pltpu.VMEM((blocks, BASE, n), F32),
        pltpu.VMEM((blocks, 1, n), F32),
    ]
    return pl.pallas_call(
        functools.partial(mixer_kernel, ns, nh),
        grid=(heads // g,),
        in_specs=[
            pl.BlockSpec((tokens, g, width), lambda i: (0, i, 0)),
            by_token(k.shape[2]),
            by_token(k.shape[2]),
            pl.BlockSpec(initial_state.shape, lambda i: (0, 0, 0)),
        ],
        out_specs=pl.BlockSpec((heads, tokens, width), lambda i: (0, 0, 0)),
        out_shape=jax.ShapeDtypeStruct((heads, tokens, width), BF16),
        scratch_shapes=[
            pltpu.VMEM((heads, tokens, width), F32),
            pltpu.VMEM((heads, tokens, width), F32),
            *maps(heads),
            *maps(heads),
            *maps(heads),
            *maps(slots, ns),
            pltpu.VMEM((slots, ns, width, width), BF16),
            pltpu.VMEM((heads, width, width), BF16),
            pltpu.VMEM((heads, width, width), BF16),
            pltpu.VMEM((slots, width, width), F32),
            dma((heads,)),
            dma((heads,)),
            dma((heads,)),
            dma((heads,)),
            dma((slots, ns)),
            dma((slots, ns)),
            dma((slots, ns)),
            dma((heads,)),
            dma((heads,)),
            dma((initial_state.shape[0],)),
            dma((slots,)),
            pltpu.VMEM((tokens * g, width), F32),
            *stage * (g // UNIT),
        ],
        compiler_params=pltpu.CompilerParams(
            collective_id=0, has_side_effects=True, vmem_limit_bytes=VMEM_BYTES
        ),
        name="mixer",
    )(q, k, v, initial_state)


def owned_per_device(queries, keys, values, initial_state):
    tokens, heads, width = queries.shape
    return jnp.swapaxes(mixer(queries, keys, values, initial_state), 0, 1)


HIGH = lax.Precision.HIGHEST


def shifted(value, axis, by):
    size = lax.axis_size(axis)
    pairs = [(i, i + by) for i in range(size) if 0 <= i + by < size]
    return lax.ppermute(value, axis, pairs)


def matmul(left, right):
    return jnp.dot(left, right, precision=HIGH, preferred_element_type=jnp.float32)


def batched(left, right):
    return jnp.einsum("hij,hjk->hik", left, right, precision=HIGH)


def unit_rows(raw_keys):
    floats = raw_keys.astype(jnp.float32)
    return floats * lax.rsqrt(jnp.sum(floats * floats, axis=-1, keepdims=True) + 1e-06)


def all_factors(k_blocks, v_blocks):
    updates = k_blocks.shape[2]
    head_width = k_blocks.shape[3]
    gram = jnp.einsum("hbid,hbjd->hbij", k_blocks, k_blocks, precision=HIGH)
    system = jnp.eye(updates, dtype=jnp.float32) + jnp.tril(2.0 * gram, -1)
    solved = lax.linalg.triangular_solve(
        system,
        2.0 * jnp.concatenate([k_blocks, v_blocks], axis=-1),
        left_side=True,
        lower=True,
        unit_diagonal=True,
    )
    return (solved[..., :head_width], solved[..., head_width:])


def visible_scores(q_blk, k_blk):
    rows = q_blk.shape[0]
    updates = k_blk.shape[0]
    per_token = updates // rows
    row_ids = lax.broadcasted_iota(jnp.int32, (rows, updates), 0)
    col_ids = lax.broadcasted_iota(jnp.int32, (rows, updates), 1)
    return jnp.where(col_ids < (row_ids + 1) * per_token, matmul(q_blk, k_blk.T), 0.0)


def start_pair(head_width):
    return jnp.concatenate(
        [jnp.zeros((head_width, head_width), jnp.float32), jnp.eye(head_width, dtype=jnp.float32)],
        axis=1,
    )


def carried_pass(q_blocks, k_blocks, w_blocks, u_blocks):
    head_width = q_blocks.shape[2]

    def advance(pair_state, block_item):
        q_blk, k_blk, w_mat, u_mat = block_item
        feed_rows = jnp.concatenate([u_mat, jnp.zeros_like(u_mat)], axis=1) - matmul(
            w_mat, pair_state
        )
        outputs = matmul(q_blk, pair_state) + matmul(visible_scores(q_blk, k_blk), feed_rows)
        return (pair_state + matmul(k_blk.T, feed_rows), outputs)

    final_pair, outputs = lax.scan(
        advance, start_pair(head_width), (q_blocks, k_blocks, w_blocks, u_blocks)
    )
    outputs = outputs.reshape(-1, 2 * head_width)
    return (
        final_pair[:, head_width:],
        final_pair[:, :head_width],
        outputs[:, :head_width],
        outputs[:, head_width:],
    )


def per_device(queries, keys, values, initial_state):
    q_heads, k_heads, v_heads = (
        lax.all_to_all(queries, "head", split_axis=1, concat_axis=0, tiled=True),
        lax.all_to_all(keys, "head", split_axis=1, concat_axis=0, tiled=True),
        lax.all_to_all(values, "head", split_axis=1, concat_axis=0, tiled=True),
    )
    head_width = q_heads.shape[2]
    local_heads = q_heads.shape[1]
    blocks = q_heads.shape[0] // BLOCK
    q_blocks = jnp.moveaxis(q_heads.astype(jnp.float32), 1, 0).reshape(
        local_heads, blocks, BLOCK, head_width
    )
    k_blocks = jnp.moveaxis(unit_rows(k_heads), 1, 0).reshape(local_heads, blocks, -1, head_width)
    v_blocks = jnp.moveaxis(v_heads.astype(jnp.float32), 1, 0).reshape(
        local_heads, blocks, -1, head_width
    )
    w_blocks, u_blocks = all_factors(k_blocks, v_blocks)
    transition, additive, local_out, query_gain = jax.vmap(carried_pass)(
        q_blocks, k_blocks, w_blocks, u_blocks
    )
    at_first = lax.axis_index("seq") == 0
    start_state = jnp.where(at_first, initial_state, jnp.zeros_like(initial_state))

    def relay_step(loop_step, current):
        passed = shifted(batched(transition, current) + additive, "seq", 1)
        return jnp.where(at_first, initial_state, passed)

    incoming = lax.fori_loop(0, lax.axis_size("seq") - 1, relay_step, start_state)
    raw_out = local_out + batched(query_gain, incoming)
    scaled = raw_out * lax.rsqrt(jnp.mean(raw_out * raw_out, axis=-1, keepdims=True) + 1e-06)
    tokens_major = jnp.moveaxis(scaled.astype(jnp.bfloat16), 0, 1)
    return lax.all_to_all(tokens_major, "head", split_axis=0, concat_axis=1, tiled=True)


def solution(mesh):
    placed = (
        P(("seq", "head"), None, None),
        P(("seq", "head"), None, None, None),
        P(("seq", "head"), None, None, None),
        P("head", None, None),
    )

    def chosen(queries, keys, values, initial_state):
        own_heads = initial_state.shape[0]
        ns, nh = mesh.shape["seq"], mesh.shape["head"]
        fits = own_heads % HEADS_A_STEP == 0 and own_heads * nh % (2 * ns) == 0
        if fits and nh > 1:
            return owned_per_device(queries, keys, values, initial_state)
        return per_device(queries, keys, values, initial_state)

    return jax.shard_map(
        chosen,
        mesh=mesh,
        in_specs=placed,
        out_specs=P(("seq", "head"), None, None),
        check_vma=False,
    )
```

```python
import functools
import itertools

import jax
import jax.numpy as jnp
from jax import lax
from jax.experimental import pallas as pl
from jax.experimental.pallas import tpu as pltpu
from jax.sharding import PartitionSpec as P

BLOCK = 64
BASE = 16
HEADS_A_STEP = 8
UNIT = 4
GROUP = 4
GRAM_SHARE = 0.25
BASE_SHARE = 1.15
VMEM_BYTES = 56 << 20

F32 = jnp.float32
BF16 = jnp.bfloat16
MESH = pl.DeviceIdType.MESH


def mm(left, right, dims=((1,), (0,))):
    return lax.dot_general(left, right, (dims, ((), ())), preferred_element_type=F32)


def split(x):
    high = x.astype(BF16)
    return high, (x - high.astype(F32)).astype(BF16)


def cat(parts, axis):
    return jnp.concatenate(parts, axis=axis)


def exact_left(left, right):
    high, low = split(right)
    return mm(cat([left, left], 1), cat([high, low], 0))


def exact_right(left, right):
    high, low = split(left)
    return mm(cat([high, low], 1), cat([right, right], 0))


def both_split(lh, ll, rh, rl):
    return mm(cat([lh, ll], 1), cat([rh, rh], 0)) + mm(lh, rl)


def both(left, right):
    return both_split(*split(left), *split(right))


def odd_rows(x, size):
    rows = x.shape[0]
    return cat([x[s : s + size] for s in range(size, rows, 2 * size)], 0)


def merge_rows(even_from, odd, size):
    rows = even_from.shape[0]
    parts = []
    for i, s in enumerate(range(0, rows, 2 * size)):
        parts += [even_from[s : s + size], odd[i * size : (i + 1) * size]]
    return cat(parts, 0)


def twice(pair, right_high, right_low):
    k = right_high.shape[0]
    return mm(pair, cat([right_high, right_high], 0)) + mm(pair[:, :k], right_low)


def grams(q_ref, k_ref, v_ref, q_rows, picked, kq_ref, v_own, x_ref, m_ref, d_ref, seen_ref):
    tokens, size, width = q_ref.shape
    per_token = k_ref.shape[2]
    step = min(BLOCK, tokens)
    n = step * per_token
    row = lax.broadcasted_iota(jnp.int32, (n, n), 0)
    col = lax.broadcasted_iota(jnp.int32, (n, n), 1)
    trow = lax.broadcasted_iota(jnp.int32, (step, n), 0)
    tcol = lax.broadcasted_iota(jnp.int32, (step, n), 1)
    visible = tcol < (trow + 1) * per_token
    for b in range(tokens // step):
        if picked[0] == 0:
            q = q_ref[b * step : (b + 1) * step].astype(F32)
            q_rows[b * step * size : (b + 1) * step * size] = q.reshape(-1, width)
        for j, h in enumerate(picked):
            i = b * len(picked) + j
            here = slice(b * step, (b + 1) * step)
            k = k_ref[here, h].reshape(n, width)
            q = q_rows[pl.ds(b * step * size + h, step, stride=size)]
            kq = cat([k, q.astype(BF16)], 0)
            kq_ref[i] = kq
            v_own[i] = v_ref[here, h].reshape(n, width)
            gs = mm(kq, k, ((1,), (1,)))
            gram = gs[:n]
            diag = jnp.where(row == col, gram, 0.0)
            norm = jnp.sum(diag, axis=1, keepdims=True) + 1e-06
            d_ref[i] = lax.rsqrt(jnp.sum(diag, axis=0, keepdims=True) + 1e-06)
            d_col = lax.rsqrt(norm)
            x = jnp.where(col < row, (2.0 * d_col * d_col) * gram, 0.0)
            x_ref[i] = cat(split(x), 1)
            seen_ref[i] = cat(split(jnp.where(visible, gs[n:], 0.0)), 1)
            packed = jnp.where(col[:BASE] < BASE, x[:BASE], 0.0)
            for s in range(BASE, n, BASE):
                inside = (col[:BASE] >= s) & (col[:BASE] < s + BASE)
                packed = jnp.where(inside, x[s : s + BASE], packed)
            m_ref[i] = packed
            yield


def base_inverses(m_ref):
    blocks, _, n = m_ref.shape
    sub = lax.broadcasted_iota(jnp.int32, (BASE, n), 0)
    lane = lax.broadcasted_iota(jnp.int32, (BASE, n), 1)
    invs = [jnp.where(sub == lane % BASE, 1.0, 0.0)] * blocks
    for j in range(BASE - 1):
        at = lane - lane % BASE + j
        for i in range(blocks):
            coef = jnp.take_along_axis(m_ref[i], at, axis=1)
            invs[i] = invs[i] - coef * invs[i][j : j + 1]
            if i % GROUP == GROUP - 1:
                yield
    for i, inv in enumerate(invs):
        m_ref[i] = inv


def inverses(v_own, x_ref, m_ref, d_ref, near_ref, fed_ref):
    blocks, n, _ = near_ref.shape
    row = lax.broadcasted_iota(jnp.int32, (n, n), 0)
    col = lax.broadcasted_iota(jnp.int32, (n, n), 1)
    same = row // BASE == col // BASE
    every = range(blocks)
    ms = [jnp.where(same, cat([m_ref[i]] * (n // BASE), 0), 0.0) for i in every]
    size = BASE
    while size < n:
        near = odd_rows(col // size - row // size, size) == -1
        halves, ys = [], []
        for i in every:
            halves.append(split(ms[i]))
            ys.append(twice(odd_rows(x_ref[i], size), *halves[i]))
            if i % GROUP == GROUP - 1:
                yield
        for i in every:
            y = jnp.where(near, ys[i], 0.0)
            ys[i] = split(merge_rows(jnp.zeros((n, n), F32), y, size))
            if i % GROUP == GROUP - 1:
                yield
        for i in every:
            mh, ml = halves[i]
            z = both_split(odd_rows(mh, size), odd_rows(ml, size), *ys[i])
            ms[i] = merge_rows(ms[i], odd_rows(ms[i], size) - z, size)
            if i % GROUP == GROUP - 1:
                yield
        size *= 2
    for i in every:
        d = d_ref[i]
        fed_ref[i] = exact_right(ms[i] * (2.0 * d), v_own[i])
        near_ref[i] = cat(split(ms[i] * (2.0 * d * d)), 1)
        if i % GROUP == GROUP - 1:
            yield


def local_maps(
    heads, kq_ref, near_ref, fed_ref, seen_ref, local_ref, gain_ref, t_ref, a_ref, first
):
    _, rows, width = kq_ref.shape
    n = near_ref.shape[1]
    step = rows - n
    count = kq_ref.shape[0] // heads
    row = lax.broadcasted_iota(jnp.int32, (width, width), 0)
    col = lax.broadcasted_iota(jnp.int32, (width, width), 1)
    eye = jnp.where(row == col, 1.0, 0.0)
    pairs = [cat([jnp.zeros((width, width), F32), eye], 1)] * heads
    for b in range(count):
        at = range(b * heads, (b + 1) * heads)
        if b == 0:
            passed, feeds = [], []
            for i in at:
                kq = kq_ref[i]
                q = kq[n:].astype(F32)
                passed.append(cat([jnp.zeros_like(q), q], 1))
                feeds.append(cat([fed_ref[i], -mm(near_ref[i], cat([kq[:n], kq[:n]], 0))], 1))
                yield
        else:
            aheads = []
            for i, pair in zip(at, pairs):
                aheads.append(exact_left(kq_ref[i], pair))
                yield
            passed = [ahead[n:] for ahead in aheads]
            feeds = []
            for i, ahead in zip(at, aheads):
                fed = cat([fed_ref[i], jnp.zeros((n, width), F32)], 1)
                feeds.append(fed - twice(near_ref[i], *split(ahead[:n])))
                yield
        feeds = [split(feed) for feed in feeds]
        made = []
        for i, pair, feed in zip(at, pairs, feeds):
            k = kq_ref[i, :n]
            made.append(pair + mm(cat([k, k], 0), cat(list(feed), 0), ((0,), (0,))))
            yield
        pairs = made
        for h, (i, base, feed) in enumerate(zip(at, passed, feeds)):
            out = base + twice(seen_ref[i], *feed)
            local_ref[first + h, b * step : (b + 1) * step] = out[:, :width]
            gain_ref[first + h, b * step : (b + 1) * step] = out[:, width:]
            yield
    for h, pair in enumerate(pairs):
        t_ref[first + h] = pair[:, width:]
        a_ref[first + h] = pair[:, :width].astype(a_ref.dtype)


def weave(mains, sides, share):
    owed = 0.0
    for _ in mains:
        owed += share
        while owed >= 1.0:
            owed -= 1.0
            next(sides, None)


def landed(ref, at, sem):
    pltpu.make_async_copy(ref.at[at], ref.at[at], sem.at[at]).wait()


def mixer_kernel(
    ns,
    nh,
    q_ref,
    k_ref,
    v_ref,
    init_ref,
    out_ref,
    local,
    gain,
    t_own,
    a_own,
    t_box,
    a_box,
    t_out,
    a_out,
    t_line,
    a_line,
    s_line,
    s_in,
    s_fwd,
    init_box,
    t_send,
    a_send,
    t_recv,
    a_recv,
    tl_recv,
    al_recv,
    sl_send,
    s_send,
    s_recv,
    i_send,
    i_recv,
    q_rows,
    *stages,
):
    size, width = q_ref.shape[1], q_ref.shape[2]
    heads = out_ref.shape[0]
    step = pl.program_id(0)
    s, z = lax.axis_index("seq"), lax.axis_index("head")
    n = ns * nh
    me = s * nh + z
    way = UNIT // 2
    ticks = heads // UNIT
    ends = (0, nh - 1)
    at_end = (z == 0) | (z == nh - 1)

    def place(p):
        return p // nh, lax.rem(p, nh)

    def head_of(group, up, j):
        return group * UNIT + up * way + j

    def slot_of(group, j):
        index = group * way + j
        turn = lax.rem(index, ns)
        half = turn // 2
        return jnp.where(lax.rem(turn, 2) == 0, half, ns - 1 - half), index // ns

    def remote(src, dst, send, recv, where):
        return pltpu.make_async_remote_copy(
            src_ref=src,
            dst_ref=dst,
            send_sem=send,
            recv_sem=recv,
            device_id=where,
            device_id_type=MESH,
        )

    def hop(h, up, t_src, a_src):
        where = (s, z + 1 if up else z - 1)
        return [
            remote(t_src.at[h], t_box.at[h], t_send.at[h], t_recv.at[h], where),
            remote(a_src.at[h], a_box.at[h], a_send.at[h], a_recv.at[h], where),
        ]

    def to_owner(h, owner, slot):
        where = (owner, z)
        return [
            remote(
                t_out.at[h], t_line.at[slot, s], t_send.at[h], tl_recv.at[slot, s], where
            ),
            remote(
                a_out.at[h], a_line.at[slot, s], a_send.at[h], al_recv.at[slot, s], where
            ),
        ]

    def from_owner(h, slot, line):
        return remote(
            s_line.at[slot, line], s_in.at[h], sl_send.at[slot, line], s_recv.at[h], (line, z)
        )

    def state_hop(h, up, src):
        where = (s, z - 1 if up else z + 1)
        return remote(src.at[h], s_in.at[h], s_send.at[h], s_recv.at[h], where)

    def place_of(up):
        return z if up else nh - 1 - z

    def group_at(tick, up):
        spot = place_of(up)
        group = tick - spot
        return group, (spot > 0) & (group >= 0) & (group < ticks)

    def join(todo):
        places = [(head_of(group, up, j), up, group, j) for group, up, j in todo]
        for h, *_ in places:
            landed(t_box, h, t_recv)
            landed(a_box, h, a_recv)
        for h, up, _, _ in places:
            if up:
                later_t, later_a, sooner_t, sooner_a = t_own, a_own, t_box, a_box
            else:
                later_t, later_a, sooner_t, sooner_a = t_box, a_box, t_own, a_own
            high, low = split(later_t[h])
            right_high, right_low = split(sooner_t[h])
            right = cat([right_high, sooner_a[h]], 1)
            made = mm(cat([high, low], 1), cat([right, right], 0))
            t_out[h] = made[:, :width] + mm(high, right_low)
            a_out[h] = (made[:, width:] + later_a[h].astype(F32)).astype(a_out.dtype)
        for h, up, group, j in places:
            spot = place_of(up)
            owner, slot = slot_of(group, j)

            @pl.when(spot < nh - 1)
            def _():
                for copy in hop(h, up, t_out, a_out):
                    copy.start()

            @pl.when((spot == nh - 1) & (owner != s) & (s < ns - 1))
            def _():
                for copy in to_owner(h, owner, slot):
                    copy.start()

            @pl.when((spot == nh - 1) & (owner == s) & (s < ns - 1))
            def _():
                pltpu.make_async_copy(
                    t_out.at[h], t_line.at[slot, s], tl_recv.at[slot, s]
                ).start()
                pltpu.make_async_copy(
                    a_out.at[h], a_line.at[slot, s], al_recv.at[slot, s]
                ).start()

    def compose(tick):
        (down, down_on), (raised, up_on) = group_at(tick, 0), group_at(tick, 1)

        @pl.when(down_on & up_on)
        def _():
            join([(raised, 1, j) for j in range(way)] + [(down, 0, j) for j in range(way)])

        @pl.when(down_on & ~up_on)
        def _():
            join([(down, 0, j) for j in range(way)])

        @pl.when(up_on & ~down_on)
        def _():
            join([(raised, 1, j) for j in range(way)])

    def compose_singly(tick):
        for j in range(way):
            for up in (1, 0):
                group, on = group_at(tick, up)

                @pl.when(on)
                def _():
                    join([(group, up, j)])

    def chain(tick):
        group = tick - nh
        turn = jnp.where(s < ns // 2, 2 * s, 2 * (ns - 1 - s) + 1)
        j = lax.rem(turn + ns * ticks * way - group * way, ns)

        @pl.when(at_end & (group >= 0) & (group < ticks) & (j < way))
        def _():
            slot = (group * way + j) // ns
            h = group * UNIT + jnp.where(z == 0, 0, way) + j
            landed(init_box, slot, i_recv)

            def send(line, state):
                s_line[slot, line] = state.astype(s_line.dtype)

                @pl.when(line != s)
                def _():
                    from_owner(h, slot, line).start()

                @pl.when(line == s)
                def _():
                    pltpu.make_async_copy(
                        s_line.at[slot, line], s_in.at[h], s_recv.at[h]
                    ).start()

            def advance(line, state):
                send(line, state)
                landed(t_line, (slot, line), tl_recv)
                landed(a_line, (slot, line), al_recv)
                return both(t_line[slot, line], state) + a_line[slot, line].astype(F32)

            send(ns - 1, lax.fori_loop(0, ns - 1, advance, init_box[slot], unroll=True))

    def finish(h, read):
        raw = local[h] + read
        mean = jnp.mean(raw * raw, axis=-1, keepdims=True)
        out_ref[h] = (raw * lax.rsqrt(mean + 1e-06)).astype(out_ref.dtype)

    def settled_at(tick, up):
        group = tick - 2 * nh + place_of(up)
        return [head_of(group, up, j) for j in range(way)], (group >= 0) & (group < ticks)

    def relay(tick, up):
        picked, on = settled_at(tick, up)

        @pl.when(on)
        def _():
            for h in picked:
                landed(s_in, h, s_recv)

            @pl.when(place_of(up) > 0)
            def _():
                for h in picked:
                    if up:
                        state_hop(h, up, s_in).start()
                    else:
                        state = exact_right(t_own[h], s_in[h]) + a_own[h].astype(F32)
                        s_fwd[h] = state.astype(BF16)
                        state_hop(h, up, s_fwd).start()

    def settle(tick, up):
        picked, on = settled_at(tick, up)
        moved = (place_of(up) > 0) if up else False

        if up:

            @pl.when(on & moved)
            def _():
                for h in picked:
                    state = exact_right(t_box[h], s_in[h]) + a_box[h].astype(F32)
                    finish(h, both(gain[h], state))

        @pl.when(on & ~moved if up else on)
        def _():
            for h in picked:
                finish(h, exact_right(gain[h], s_in[h]))

    def exchange(tick, pieces=compose):
        chain(tick)
        pieces(tick)
        for up in (1, 0):
            relay(tick, up)
        for up in (1, 0):
            settle(tick, up)

    own = init_ref.shape[0]

    def init_copies():
        for i in range(own):
            h = z * own + i
            up = (i % UNIT) // way
            owner, slot = slot_of(h // UNIT, i % way)
            copy = remote(
                init_ref.at[i], init_box.at[slot], i_send.at[i], i_recv.at[slot], (s, ends[up])
            )
            yield i, up, owner, slot, copy

    @pl.when(step == 0)
    def _():
        barrier = pltpu.get_barrier_semaphore()

        @pl.loop(1, n)
        def _(i):
            pl.semaphore_signal(
                barrier, inc=1, device_id=place(lax.rem(me + i, n)), device_id_type=MESH
            )

    subs = size // UNIT
    kept = len(stages) // subs

    def stage_of(sub):
        return stages[sub * kept : (sub + 1) * kept]

    def picked_of(sub):
        return list(range(sub * UNIT, (sub + 1) * UNIT))

    def advance_maps(done, first, later):
        none = iter(())
        invert, carry, gram, base = none, none, none, none
        if done is not None:
            kq, near, fed, seen, v_own, x, m, d = stage_of(done)
            invert = inverses(v_own, x, m, d, near, fed)
            carry = local_maps(
                UNIT, kq, near, fed, seen, local, gain, t_own, a_own, first
            )
        if later is not None:
            kq, near, fed, seen, v_own, x, m, d = stage_of(later)
            gram = grams(
                q_ref, k_ref, v_ref, q_rows, picked_of(later), kq, v_own, x, m, d, seen
            )
            base = base_inverses(m)
        sides = itertools.chain(gram, base)
        weave(invert, sides, GRAM_SHARE)
        weave(carry, sides, BASE_SHARE)
        for _ in sides:
            pass

    def offer(first):
        for up in (0, 1):

            @pl.when(place_of(up) == 0)
            def _():
                for j in range(way):
                    for copy in hop(first + up * way + j, up, t_own, a_own):
                        copy.start()

    @pl.when(step == 0)
    def _():
        advance_maps(None, None, 0)
        pl.semaphore_wait(pltpu.get_barrier_semaphore(), n - 1)
        for i, up, owner, slot, copy in init_copies():

            @pl.when((owner == s) & (z != ends[up]))
            def _():
                copy.start()

            @pl.when((owner == s) & (z == ends[up]))
            def _():
                pltpu.make_async_copy(
                    init_ref.at[i], init_box.at[slot], i_recv.at[slot]
                ).start()

    @pl.when(step > 0)
    def _():
        advance_maps(subs - 1, step * size - UNIT, 0)
        offer(step * size - UNIT)
        exchange(step * subs - 1)

    for sub in range(1, subs):
        advance_maps(sub - 1, step * size + (sub - 1) * UNIT, sub)
        offer(step * size + (sub - 1) * UNIT)
        exchange(step * subs + sub - 1)

    @pl.when(step == pl.num_programs(0) - 1)
    def _():
        advance_maps(subs - 1, heads - UNIT, None)
        offer(heads - UNIT)

        @pl.loop(ticks - 1, ticks + 2 * nh)
        def _(tick):
            exchange(tick, compose_singly)

        for i, up, owner, slot, copy in init_copies():

            @pl.when((owner == s) & (z != ends[up]))
            def _():
                copy.wait_send()

        @pl.loop(0, ticks)
        def _(group):
            for up in (0, 1):
                spot = place_of(up)
                for j in range(way):
                    h = head_of(group, up, j)
                    owner, slot = slot_of(group, j)

                    @pl.when(spot < nh - 1)
                    def _():
                        for copy in hop(h, up, t_out, a_out):
                            copy.wait_send()

                    @pl.when((spot == nh - 1) & (owner != s) & (s < ns - 1))
                    def _():
                        for copy in to_owner(h, owner, slot):
                            copy.wait_send()

                    @pl.when(spot > 0)
                    def _():
                        state_hop(h, up, s_fwd).wait_send()

                    @pl.when((spot == nh - 1) & (owner == s))
                    def _():
                        @pl.loop(0, ns)
                        def _(line):
                            @pl.when(line != s)
                            def _():
                                from_owner(h, slot, line).wait_send()


def mixer(q, k, v, initial_state):
    ns, nh = lax.axis_size("seq"), lax.axis_size("head")
    tokens, heads, width = q.shape
    g = HEADS_A_STEP
    slots = heads // (2 * ns)
    dma = pltpu.SemaphoreType.DMA

    def by_token(rows):
        return pl.BlockSpec((tokens, g, rows, width), lambda i: (0, i, 0, 0))

    def maps(*lead):
        square = (*lead, width, width)
        return [pltpu.VMEM(square, F32), pltpu.VMEM(square, BF16)]

    step = min(BLOCK, tokens)
    n = step * k.shape[2]
    blocks = UNIT * (tokens // step)
    stage = [
        pltpu.VMEM((blocks, n + step, width), BF16),
        pltpu.VMEM((blocks, n, 2 * n), BF16),
        pltpu.VMEM((blocks, n, width), F32),
        pltpu.VMEM((blocks, step, 2 * n), BF16),
        pltpu.VMEM((blocks, n, width), BF16),
        pltpu.VMEM((blocks, n, 2 * n), BF16),
        pltpu.VMEM((blocks, BASE, n), F32),
        pltpu.VMEM((blocks, 1, n), F32),
    ]
    return pl.pallas_call(
        functools.partial(mixer_kernel, ns, nh),
        grid=(heads // g,),
        in_specs=[
            pl.BlockSpec((tokens, g, width), lambda i: (0, i, 0)),
            by_token(k.shape[2]),
            by_token(k.shape[2]),
            pl.BlockSpec(initial_state.shape, lambda i: (0, 0, 0)),
        ],
        out_specs=pl.BlockSpec((heads, tokens, width), lambda i: (0, 0, 0)),
        out_shape=jax.ShapeDtypeStruct((heads, tokens, width), BF16),
        scratch_shapes=[
            pltpu.VMEM((heads, tokens, width), F32),
            pltpu.VMEM((heads, tokens, width), F32),
            *maps(heads),
            *maps(heads),
            *maps(heads),
            *maps(slots, ns),
            pltpu.VMEM((slots, ns, width, width), BF16),
            pltpu.VMEM((heads, width, width), BF16),
            pltpu.VMEM((heads, width, width), BF16),
            pltpu.VMEM((slots, width, width), F32),
            dma((heads,)),
            dma((heads,)),
            dma((heads,)),
            dma((heads,)),
            dma((slots, ns)),
            dma((slots, ns)),
            dma((slots, ns)),
            dma((heads,)),
            dma((heads,)),
            dma((initial_state.shape[0],)),
            dma((slots,)),
            pltpu.VMEM((tokens * g, width), F32),
            *stage * (g // UNIT),
        ],
        compiler_params=pltpu.CompilerParams(
            collective_id=0, has_side_effects=True, vmem_limit_bytes=VMEM_BYTES
        ),
        name="mixer",
    )(q, k, v, initial_state)


def owned_per_device(queries, keys, values, initial_state):
    tokens, heads, width = queries.shape
    return jnp.swapaxes(mixer(queries, keys, values, initial_state), 0, 1)


HIGH = lax.Precision.HIGHEST


def shifted(value, axis, by):
    size = lax.axis_size(axis)
    pairs = [(i, i + by) for i in range(size) if 0 <= i + by < size]
    return lax.ppermute(value, axis, pairs)


def matmul(left, right):
    return jnp.dot(left, right, precision=HIGH, preferred_element_type=jnp.float32)


def batched(left, right):
    return jnp.einsum("hij,hjk->hik", left, right, precision=HIGH)


def unit_rows(raw_keys):
    floats = raw_keys.astype(jnp.float32)
    return floats * lax.rsqrt(jnp.sum(floats * floats, axis=-1, keepdims=True) + 1e-06)


def all_factors(k_blocks, v_blocks):
    updates = k_blocks.shape[2]
    head_width = k_blocks.shape[3]
    gram = jnp.einsum("hbid,hbjd->hbij", k_blocks, k_blocks, precision=HIGH)
    system = jnp.eye(updates, dtype=jnp.float32) + jnp.tril(2.0 * gram, -1)
    solved = lax.linalg.triangular_solve(
        system,
        2.0 * jnp.concatenate([k_blocks, v_blocks], axis=-1),
        left_side=True,
        lower=True,
        unit_diagonal=True,
    )
    return (solved[..., :head_width], solved[..., head_width:])


def visible_scores(q_blk, k_blk):
    rows = q_blk.shape[0]
    updates = k_blk.shape[0]
    per_token = updates // rows
    row_ids = lax.broadcasted_iota(jnp.int32, (rows, updates), 0)
    col_ids = lax.broadcasted_iota(jnp.int32, (rows, updates), 1)
    return jnp.where(col_ids < (row_ids + 1) * per_token, matmul(q_blk, k_blk.T), 0.0)


def start_pair(head_width):
    return jnp.concatenate(
        [jnp.zeros((head_width, head_width), jnp.float32), jnp.eye(head_width, dtype=jnp.float32)],
        axis=1,
    )


def carried_pass(q_blocks, k_blocks, w_blocks, u_blocks):
    head_width = q_blocks.shape[2]

    def advance(pair_state, block_item):
        q_blk, k_blk, w_mat, u_mat = block_item
        feed_rows = jnp.concatenate([u_mat, jnp.zeros_like(u_mat)], axis=1) - matmul(
            w_mat, pair_state
        )
        outputs = matmul(q_blk, pair_state) + matmul(visible_scores(q_blk, k_blk), feed_rows)
        return (pair_state + matmul(k_blk.T, feed_rows), outputs)

    final_pair, outputs = lax.scan(
        advance, start_pair(head_width), (q_blocks, k_blocks, w_blocks, u_blocks)
    )
    outputs = outputs.reshape(-1, 2 * head_width)
    return (
        final_pair[:, head_width:],
        final_pair[:, :head_width],
        outputs[:, :head_width],
        outputs[:, head_width:],
    )


def per_device(queries, keys, values, initial_state):
    q_heads, k_heads, v_heads = (
        lax.all_to_all(queries, "head", split_axis=1, concat_axis=0, tiled=True),
        lax.all_to_all(keys, "head", split_axis=1, concat_axis=0, tiled=True),
        lax.all_to_all(values, "head", split_axis=1, concat_axis=0, tiled=True),
    )
    head_width = q_heads.shape[2]
    local_heads = q_heads.shape[1]
    blocks = q_heads.shape[0] // BLOCK
    q_blocks = jnp.moveaxis(q_heads.astype(jnp.float32), 1, 0).reshape(
        local_heads, blocks, BLOCK, head_width
    )
    k_blocks = jnp.moveaxis(unit_rows(k_heads), 1, 0).reshape(local_heads, blocks, -1, head_width)
    v_blocks = jnp.moveaxis(v_heads.astype(jnp.float32), 1, 0).reshape(
        local_heads, blocks, -1, head_width
    )
    w_blocks, u_blocks = all_factors(k_blocks, v_blocks)
    transition, additive, local_out, query_gain = jax.vmap(carried_pass)(
        q_blocks, k_blocks, w_blocks, u_blocks
    )
    at_first = lax.axis_index("seq") == 0
    start_state = jnp.where(at_first, initial_state, jnp.zeros_like(initial_state))

    def relay_step(loop_step, current):
        passed = shifted(batched(transition, current) + additive, "seq", 1)
        return jnp.where(at_first, initial_state, passed)

    incoming = lax.fori_loop(0, lax.axis_size("seq") - 1, relay_step, start_state)
    raw_out = local_out + batched(query_gain, incoming)
    scaled = raw_out * lax.rsqrt(jnp.mean(raw_out * raw_out, axis=-1, keepdims=True) + 1e-06)
    tokens_major = jnp.moveaxis(scaled.astype(jnp.bfloat16), 0, 1)
    return lax.all_to_all(tokens_major, "head", split_axis=0, concat_axis=1, tiled=True)


def solution(mesh):
    placed = (
        P(("seq", "head"), None, None),
        P(("seq", "head"), None, None, None),
        P(("seq", "head"), None, None, None),
        P("head", None, None),
    )

    def chosen(queries, keys, values, initial_state):
        own_heads = initial_state.shape[0]
        ns, nh = mesh.shape["seq"], mesh.shape["head"]
        fits = own_heads % HEADS_A_STEP == 0 and own_heads * nh % (2 * ns) == 0
        if fits and nh > 1:
            return owned_per_device(queries, keys, values, initial_state)
        return per_device(queries, keys, values, initial_state)

    return jax.shard_map(
        chosen,
        mesh=mesh,
        in_specs=placed,
        out_specs=P(("seq", "head"), None, None),
        check_vma=False,
    )
```
